128 devices in a mesh: seq: 16 (over y, z), tp: 8 (over x, core).
Axes of the slice: x: 4, y: 4, z: 4, core: 2. Of those that a mesh axis runs over, the one named last changes fastest.
Arguments:
- stream_in: bfloat16 [2048, 2880], P('seq'), may hold values from -40 to 40
- attn_gain: float32 [2880], replicated, may hold values from 0.1 to 1.9
- w_qkv: bfloat16 [2880, 8, 640], P(None, 'tp'), may hold values from -2 to 2
- key_value_cache: bfloat16 [128, 8, 128], P(None, 'tp'), may hold values from -6 to 6
- w_out: bfloat16 [4096, 2880], P('tp'), may hold values from -0.09375 to 0.09375
- mlp_gain: float32 [2880], replicated, may hold values from 0.1 to 1.9
- expert_index: int32 [2048, 4], P(('seq', 'tp')), may hold values from 0 to 31, all different within a row; in each aligned block of 16 rows (0 to 15, 16 to 31, ...) at most 4 rows name the same one
- gate_weight: float32 [2048, 4], P(('seq', 'tp')), may hold values from 0.05 to 0.5
- w_gateup: bfloat16 [32, 2880, 2, 2880], P('seq', None, None, 'tp'), may hold values from -0.109375 to 0.109375
- w_down: bfloat16 [32, 2880, 2880], P('seq', 'tp'), may hold values from -0.109375 to 0.109375
Outputs:
- stream_out: bfloat16 [2048, 2880], P(('seq', 'tp'))
The draws below stay inside these ranges and needn't reach their ends.
Inputs may be any that keep to these rules, and one draw needn't show every extreme that they name: `expert_index`: in the rows of one device (aligned blocks of 16 rows) no expert is named by more than 4 rows, a bound that some block reaches; a row names 4 different experts.
All inputs are finite; a program needn't handle non-finite values.
Results may differ from the reference program's by a relative error of at most 0.01.
Values may be sent and summed in bfloat16 or wider, within the bound.
A program may use at most 128 MiB of HBM per device.

```python
import math
import jax
import jax.numpy as jnp
import numpy as np
from jax import lax

MODEL_WIDTH = 2880
QUERY_HEADS = 64
KEY_VALUE_HEADS = 8
HEAD_SIZE = 64
WINDOW_KEYS = 128
EXPERTS = 32
FFE = 2880
TOPK = 4
TOK_DEV = 128
BLOCK_TOKENS = 2048
CAP = 4
N_SEQ = 16
N_TP = 8


def draw_stream_in(key, part):
    root_random_key = jax.random.fold_in(jax.random.fold_in(key, 11), 0)
    values = jax.random.normal(root_random_key, (BLOCK_TOKENS, MODEL_WIDTH), jnp.float32)
    return jnp.clip(values, -40.0, 40.0).astype(jnp.bfloat16)


def draw_w_qkv(key, part):
    root_random_key = jax.random.fold_in(jax.random.fold_in(key, 23), 0)
    query_group_width = QUERY_HEADS // KEY_VALUE_HEADS
    layer_weights = jax.random.normal(root_random_key, (MODEL_WIDTH, KEY_VALUE_HEADS, query_group_width + 2, HEAD_SIZE), jnp.float32) * MODEL_WIDTH ** (-0.5)
    layer_weights = jnp.clip(layer_weights, -2.0, 2.0)
    return layer_weights.reshape(MODEL_WIDTH, KEY_VALUE_HEADS, (query_group_width + 2) * HEAD_SIZE).astype(jnp.bfloat16)


def levels(key, shape, pieces, smallest, high):
    def one(dim, shards_of):
        steps = jax.random.uniform(jax.random.fold_in(jax.random.fold_in(key, 6), dim), (shards_of,), jnp.float32, smallest / len(pieces), high / len(pieces))
        return jnp.repeat(jnp.exp(steps), shape[dim] // shards_of).reshape((-1,) + (1,) * (len(shape) - dim - 1))

    loudness = one(*pieces[0])
    for cut in pieces[1:]:
        loudness = loudness * one(*cut)
    return loudness


def assign_block(stream_key, own, number, rows, count, top, reach, slope):
    sequence = jax.random.permutation(stream_key, count)
    packed, common = portions_of(count, rows * top, reach, slope, True), portions_of(count, rows * top, reach, slope, False)
    places = jnp.arange(count)

    def named(sizes, turn):
        used = int((sizes > 0).sum())
        fixed = max(1, used // 4)
        passed = fixed + (places - fixed + turn * (used - fixed)) % max(1, count - fixed)
        return jnp.zeros((count,), jnp.int32).at[sequence[jnp.where(places < fixed, places, passed)]].set(jnp.asarray(sizes, jnp.int32))

    sizes = jnp.where(number % 4 == 0, named(packed, number // 4), named(common, number - number // 4 - 1))
    mixed = jax.random.permutation(jax.random.fold_in(own, 3), count)
    source_of, taker = mixed[0:count // 2 * 2:2], mixed[1:count // 2 * 2:2]
    slack = jnp.minimum(sizes[source_of] - 1, reach - sizes[taker]) // 2
    slack = jnp.where((source_of == sequence[0]) | (taker == sequence[0]) | (sizes[taker] == 0), 0, jnp.maximum(slack, 0))
    passed = jax.random.randint(jax.random.fold_in(own, 4), (count // 2,), 0, 1 << 20) % (slack + 1)
    sizes = sizes.at[source_of].add(-passed).at[taker].add(passed)
    items = jnp.searchsorted(jnp.cumsum(sizes), jnp.arange(rows * top), side="right").astype(jnp.int32)
    grid = items.reshape(top, rows).T
    grid = grid[jax.random.permutation(jax.random.fold_in(own, 1), rows)]
    turn = jax.random.randint(jax.random.fold_in(own, 2), (rows, 1), 0, top)
    return jnp.take_along_axis(grid, (jnp.arange(top)[None, :] + turn) % top, axis=1)


def portions_of(count, total, bound, skew, full):
    weights = [(1 << 20) // math.isqrt(standing ** skew) + 1 for standing in range(1, count + 1)]
    largest = bound if full else min(bound, max(-(-total // count), total * weights[0] // sum(weights)))
    least = 1 if total - largest >= count - 1 else 0
    holding, surplus = [largest] + [least] * (count - 1), total - largest - least * (count - 1)
    while surplus > 0:
        movable = [i for i in range(1, count) if holding[i] < largest] or [i for i in range(1, count) if holding[i] < bound]
        pool, remaining = sum([weights[i] for i in movable]), surplus
        for i in movable:
            addition = min(bound - holding[i], max(1, remaining * weights[i] // pool), surplus)
            holding[i] = holding[i] + addition
            surplus = surplus - addition
    return np.array(holding)


def bell_draw(stream_key, dims, spread, most, pieces=(), kind=jnp.bfloat16):
    entries = spread * jax.random.normal(stream_key, dims, jnp.float32)
    if pieces:
        entries = entries * levels(stream_key, dims, pieces, -0.22, 0.18)
    return jnp.clip(entries, -most, most).astype(kind)


def setup_inputs(seed: int = 0) -> dict:
    key_list = jax.random.split(jax.random.key(seed), 11)
    stream_in = draw_stream_in(jax.random.fold_in(key_list[10], 71), 0)
    attn_gain = jnp.clip(1.0 + 0.18 * jax.random.normal(key_list[1], (MODEL_WIDTH,), jnp.float32), 0.1, 1.9)
    w_qkv = draw_w_qkv(jax.random.fold_in(key_list[10], 71), 0)
    key_value_cache = bell_draw(key_list[3], (WINDOW_KEYS, KEY_VALUE_HEADS, 2 * HEAD_SIZE), 1.0, 6.0, ((1, 8),))
    w_out = bell_draw(key_list[4], (QUERY_HEADS * HEAD_SIZE, MODEL_WIDTH), (QUERY_HEADS * HEAD_SIZE) ** -0.5, 0.09375, ((0, 8),))
    mlp_gain = jnp.clip(1.0 + 0.18 * jax.random.normal(key_list[5], (MODEL_WIDTH,), jnp.float32), 0.1, 1.9)
    expert_index_keys = jax.random.split(jax.random.fold_in(key_list[6], 1), BLOCK_TOKENS // (TOK_DEV // N_TP))
    expert_index_turns = jax.random.permutation(jax.random.fold_in(key_list[6], 3), BLOCK_TOKENS // (TOK_DEV // N_TP))
    expert_index = jax.vmap(lambda own, number: assign_block(jax.random.fold_in(key_list[6], 2), own, number, TOK_DEV // N_TP, EXPERTS, TOPK, CAP, 2))(expert_index_keys, expert_index_turns).reshape((BLOCK_TOKENS, TOPK))
    gate_weight = jnp.clip(0.05 + 0.45 * jax.random.uniform(key_list[7], (BLOCK_TOKENS, TOPK), jnp.float32) ** levels(key_list[7], (BLOCK_TOKENS, TOPK), ((0, 128),), -0.2, 0.2), 0.05, 0.5)
    w_gateup = bell_draw(key_list[8], (EXPERTS, MODEL_WIDTH, 2, FFE), MODEL_WIDTH ** -0.5, 0.109375, ((0, 16), (3, 8)))
    w_down = bell_draw(key_list[9], (EXPERTS, FFE, MODEL_WIDTH), FFE ** -0.5, 0.109375, ((0, 16), (1, 8)))
    return {"stream_in": stream_in, "attn_gain": attn_gain, "w_qkv": w_qkv, "key_value_cache": key_value_cache, "w_out": w_out, "mlp_gain": mlp_gain, "expert_index": expert_index, "gate_weight": gate_weight, "w_gateup": w_gateup, "w_down": w_down}


EPS = 1e-05

def rms_scale(values, gain_vec):
    mean_sq = lax.optimization_barrier(jnp.mean(values * values, axis=-1, keepdims=True))
    return values * lax.rsqrt(mean_sq + EPS) * gain_vec

def window_block(queries, key_rows, value_rows):
    scores = jnp.einsum('qhgc,khc->hgqk', queries.astype(jnp.float32), key_rows.astype(jnp.float32)) * HEAD_SIZE ** (-0.5)
    key_offset = jnp.arange(key_rows.shape[0])[None, :] - jnp.arange(queries.shape[0])[:, None]
    in_window = (key_offset >= 1) & (key_offset <= WINDOW_KEYS)
    scores = jnp.where(in_window, scores, -1e+30)
    row_max = lax.optimization_barrier(jnp.max(scores, axis=-1, keepdims=True))
    exponent = jnp.exp(scores - row_max)
    layer_weights = (exponent / lax.optimization_barrier(jnp.sum(exponent, axis=-1, keepdims=True))).astype(jnp.bfloat16)
    attended = jnp.einsum('hgqk,khc->qhgc', layer_weights.astype(jnp.float32), value_rows.astype(jnp.float32))
    return attended.astype(jnp.bfloat16)

def reference(stream_in, attn_gain, w_qkv, key_value_cache, w_out, mlp_gain, expert_index, gate_weight, w_gateup, w_down):
    query_group_width = QUERY_HEADS // KEY_VALUE_HEADS
    normed = rms_scale(stream_in.astype(jnp.float32), attn_gain).astype(jnp.bfloat16)
    projected_rows = jnp.einsum('td,dhc->thc', normed.astype(jnp.float32), w_qkv.astype(jnp.float32)).astype(jnp.bfloat16)
    projected_rows = projected_rows.reshape(BLOCK_TOKENS, KEY_VALUE_HEADS, query_group_width + 2, HEAD_SIZE)
    queries = projected_rows[:, :, :query_group_width]
    key_rows = jnp.concatenate([key_value_cache[:, :, :HEAD_SIZE], projected_rows[:, :, query_group_width]], axis=0)
    value_rows = jnp.concatenate([key_value_cache[:, :, HEAD_SIZE:], projected_rows[:, :, query_group_width + 1]], axis=0)

    def one_block(block_index):
        row_start = (block_index * TOK_DEV).astype(jnp.int32)
        block_q = lax.dynamic_slice_in_dim(queries, row_start, TOK_DEV, 0)
        block_k = lax.dynamic_slice_in_dim(key_rows, row_start, TOK_DEV + WINDOW_KEYS, 0)
        block_v = lax.dynamic_slice_in_dim(value_rows, row_start, TOK_DEV + WINDOW_KEYS, 0)
        return window_block(block_q, block_k, block_v)
    attended = lax.map(one_block, jnp.arange(N_SEQ, dtype=jnp.int32)).reshape(BLOCK_TOKENS, QUERY_HEADS * HEAD_SIZE)
    residual = stream_in.astype(jnp.float32) + jnp.dot(attended, w_out, preferred_element_type=jnp.float32)
    hidden_in = rms_scale(residual, mlp_gain).astype(jnp.bfloat16)
    block_rows = TOK_DEV // N_TP
    blocks = BLOCK_TOKENS // block_rows
    capacity = 2 * TOK_DEV * TOPK // (N_TP * EXPERTS)
    flat_index = expert_index.reshape(blocks, block_rows * TOPK)
    onehot = (flat_index[:, :, None] == jnp.arange(EXPERTS, dtype=jnp.int32)[None, None, :]).astype(jnp.int32)
    slot_rank = lax.optimization_barrier(jnp.sum((jnp.cumsum(onehot, axis=1) - 1) * onehot, axis=2)).astype(jnp.int32)
    block_id = jnp.broadcast_to(jnp.arange(blocks, dtype=jnp.int32)[:, None], flat_index.shape)
    row_values = jnp.repeat(hidden_in.reshape(blocks, block_rows, MODEL_WIDTH), TOPK, axis=1)
    buffer = jnp.zeros((blocks, EXPERTS, capacity, MODEL_WIDTH), jnp.bfloat16).at[block_id, flat_index, slot_rank].set(row_values)
    slice_units = FFE // N_TP

    def one_expert(operands):
        chosen, gate_up_matrix, down_proj = operands
        input_rows = chosen.reshape(blocks * capacity, MODEL_WIDTH).astype(jnp.float32)
        gate_up_rows = jnp.einsum('vi,ipk->vpk', input_rows, gate_up_matrix.astype(jnp.float32))
        activated = (jax.nn.silu(gate_up_rows[:, 0]) * gate_up_rows[:, 1]).astype(jnp.bfloat16)
        partials = jnp.einsum('ltf,tfd->ltd', activated.reshape(-1, N_TP, slice_units).astype(jnp.float32), down_proj.reshape(N_TP, slice_units, MODEL_WIDTH).astype(jnp.float32))
        rounded = lax.optimization_barrier(partials.astype(jnp.bfloat16))
        total = lax.optimization_barrier(jnp.sum(rounded.astype(jnp.float32), axis=1))
        return total.astype(jnp.bfloat16).reshape(blocks, capacity, MODEL_WIDTH)
    results = lax.map(one_expert, (jnp.moveaxis(buffer, 1, 0), w_gateup, w_down))
    expert_out = results[flat_index, block_id, slot_rank].reshape(BLOCK_TOKENS, TOPK, MODEL_WIDTH)
    mixture = lax.optimization_barrier(jnp.sum(gate_weight[:, :, None] * expert_out.astype(jnp.float32), axis=1))
    return (residual + mixture).astype(jnp.bfloat16)
```

```python
import functools

import jax
import jax.numpy as jnp
from jax import lax
from jax.experimental import pallas as pl
from jax.experimental.pallas import tpu as pltpu
from jax.sharding import PartitionSpec as P

MODEL_WIDTH = 2880
QUERY_HEADS = 64
KEY_VALUE_HEADS = 8
HEAD_SIZE = 64
WINDOW_KEYS = 128
EXPERTS = 32
TOPK = 4


EPS = 1e-05


def from_behind(value, axis, steps):
    count = lax.axis_size(axis)
    first, last = (max(0, -steps), min(count, count - steps))
    return lax.ppermute(value, axis, [(source, source + steps) for source in range(first, last)])


def rms_scale(values, gain_vec):
    mean_sq = jnp.mean(values * values, axis=-1, keepdims=True)
    return values * lax.rsqrt(mean_sq + EPS) * gain_vec


def window_block(queries, key_rows, value_rows):
    scores = jnp.einsum(
        "qhgc,khc->hgqk", queries, key_rows, preferred_element_type=jnp.float32
    ) * HEAD_SIZE ** (-0.5)
    key_offset = jnp.arange(key_rows.shape[0])[None, :] - jnp.arange(queries.shape[0])[:, None]
    in_window = (key_offset >= 1) & (key_offset <= WINDOW_KEYS)
    scores = jnp.where(in_window, scores, -1e30)
    row_max = jnp.max(scores, axis=-1, keepdims=True)
    exponent = jnp.exp(scores - row_max)
    layer_weights = (exponent / jnp.sum(exponent, axis=-1, keepdims=True)).astype(jnp.bfloat16)
    attended = jnp.einsum(
        "hgqk,khc->qhgc", layer_weights, value_rows, preferred_element_type=jnp.float32
    )
    return attended.astype(jnp.bfloat16)


class Copies:
    def __init__(self, send_sems):
        self.send_sems = send_sems
        self.started = []

    def start(self, src, dst, recv_sem, seq, tp):
        copy = pltpu.make_async_remote_copy(
            src_ref=src,
            dst_ref=dst,
            send_sem=self.send_sems.at[len(self.started)],
            recv_sem=recv_sem,
            device_id=(seq, tp),
            device_id_type=pl.DeviceIdType.MESH,
        )
        copy.start()
        self.started.append(copy)

    def drain(self):
        for copy in self.started:
            copy.wait_send()


def arrived(ref, sem):
    pltpu.make_async_copy(ref, ref, sem).wait()


def moe_kernel(
    n_seq,
    n_x,
    part,
    stream_rows,
    gain,
    placer,
    picker,
    w_gateup_hbm,
    w_down_hbm,
    out,
    attn_pair,
    attn_sum,
    attn_in,
    residual,
    hidden,
    packed,
    rows,
    w_gateup,
    w_down,
    product,
    from_pair,
    chip_sum,
    ring_opp,
    ring_in,
    final,
    returned,
    mixed,
    mixed_in,
    load_sems,
    send_sems,
    attn_sems,
    block_sems,
    ring_sems,
    pair_sems,
    back_sems,
):
    seq, tp = lax.axis_index("seq"), lax.axis_index("tp")
    x, core = tp // 2, tp % 2
    nz = 4 if n_seq % 4 == 0 else n_seq
    ny = n_seq // nz
    y, z = seq // nz, seq % nz
    partner = tp + 1 - 2 * core
    right_x, left_x, far_x = (x + 1) % n_x, (x + n_x - 1) % n_x, (x + 2) % n_x
    right, left, far = right_x * 2 + core, left_x * 2 + core, far_x * 2 + core
    chunk = max(1, n_seq // 4)
    chunks = n_seq // chunk
    half = chunks // 2
    half_rows = n_seq // 2
    width = out.shape[-1]
    copies = Copies(send_sems)

    loads = [
        pltpu.make_async_copy(w_gateup_hbm, w_gateup, load_sems.at[0]),
        pltpu.make_async_copy(w_down_hbm, w_down, load_sems.at[1]),
    ]
    for load in loads:
        load.start()

    def behind(slot):
        dy, dz = slot // nz, slot % nz
        return ((y + ny - dy) % ny) * nz + (z + nz - dz) % nz

    def ahead(slot):
        dy, dz = slot // nz, slot % nz
        return ((y + dy) % ny) * nz + (z + dz) % nz

    barrier = pltpu.get_barrier_semaphore()
    for slot in range(1, n_seq):
        pl.semaphore_signal(
            barrier, inc=1, device_id=(ahead(slot), tp), device_id_type=pl.DeviceIdType.MESH
        )
    for peer in (partner, right, left, far):
        pl.semaphore_signal(
            barrier, inc=1, device_id=(seq, peer), device_id_type=pl.DeviceIdType.MESH
        )
    pl.semaphore_wait(barrier, n_seq - 1 + 4)

    copies.start(part.at[1 - core], attn_pair, attn_sems.at[0], seq, partner)
    arrived(attn_pair, attn_sems.at[0])
    attn_sum[...] = (
        part[core].astype(jnp.float32) + attn_pair[...].astype(jnp.float32)
    ).astype(jnp.bfloat16)
    for step, peer_x in ((1, far_x), (0, right_x), (2, left_x)):
        copies.start(
            attn_sum.at[peer_x], attn_in.at[step], attn_sems.at[1 + step], seq, peer_x * 2 + core
        )
    total = stream_rows[...].astype(jnp.float32) + attn_sum[x].astype(jnp.float32)
    for step in range(3):
        arrived(attn_in.at[step], attn_sems.at[1 + step])
    for step in range(3):
        total = total + attn_in[step].astype(jnp.float32)
    residual[...] = total
    hidden[core] = rms_scale(total, gain[...]).astype(jnp.bfloat16)
    copies.start(hidden.at[core], hidden.at[core], attn_sems.at[4], seq, partner)
    arrived(hidden.at[1 - core], attn_sems.at[4])

    both = hidden[...].reshape(-1, width)
    packed[...] = (
        jnp.dot(placer[...], both, preferred_element_type=jnp.float32)
        .reshape(packed.shape)
        .astype(jnp.bfloat16)
    )
    for group in range(chunks):
        for slot in range(group * chunk, (group + 1) * chunk):
            if slot:
                copies.start(
                    packed.at[behind(slot)],
                    rows.at[core, x, slot],
                    block_sems.at[group],
                    behind(slot),
                    tp,
                )
    rows[core, x, 0] = packed[seq]

    def slots(group):
        return pl.ds(group * chunk, chunk)

    for group in range(chunks):
        first = 1 if group == 0 else 0
        if chunk > first:
            got = rows.at[core, x, pl.ds(group * chunk + first, chunk - first)]
            arrived(got, block_sems.at[group])
        own = rows.at[core, x, slots(group)]
        copies.start(own, own, ring_sems.at[0, group], seq, right)
        copies.start(own, own, ring_sems.at[1, group], seq, left)
        copies.start(own, own, pair_sems.at[0, group], seq, partner)

    for load in loads:
        load.wait()

    def compute(block_x):
        def one(expert, carry):
            taken = rows[expert, block_x].reshape(n_seq * 8, width)
            contract = (((1,), (1,)), ((), ()))
            gate = lax.dot_general(
                taken, w_gateup[expert, 0], contract, preferred_element_type=jnp.float32
            )
            up = lax.dot_general(
                taken, w_gateup[expert, 1], contract, preferred_element_type=jnp.float32
            )
            activated = (gate / (1.0 + jnp.exp(-gate)) * up).astype(jnp.bfloat16)
            result = jnp.dot(activated, w_down[expert], preferred_element_type=jnp.float32)
            product[expert, block_x] = result.reshape(n_seq, 8, width).astype(jnp.bfloat16)
            return carry

        lax.fori_loop(0, 2, one, 0)

    def to_pair(block_x, which):
        copies.start(
            product.at[1 - core, block_x],
            from_pair.at[block_x],
            back_sems.at[which],
            seq,
            partner,
        )

    def pair_sum(block_x, which):
        arrived(from_pair.at[block_x], back_sems.at[which])
        chip_sum[block_x] = (
            product[core, block_x].astype(jnp.float32) + from_pair[block_x].astype(jnp.float32)
        ).astype(jnp.bfloat16)

    for group in range(chunks):
        arrived(rows.at[1 - core, x, slots(group)], pair_sems.at[0, group])
    compute(x)
    to_pair(x, 0)

    for group in range(chunks):
        got = rows.at[core, left_x, slots(group)]
        arrived(got, ring_sems.at[0, group])
        if group < half:
            copies.start(got, got, ring_sems.at[2, group], seq, right)
        copies.start(got, got, pair_sems.at[1, group], seq, partner)
        got = rows.at[core, right_x, slots(group)]
        arrived(got, ring_sems.at[1, group])
        if group >= half:
            copies.start(got, got, ring_sems.at[2, group], seq, left)
        copies.start(got, got, pair_sems.at[2, group], seq, partner)
    for group in range(chunks):
        arrived(rows.at[1 - core, left_x, slots(group)], pair_sems.at[1, group])
    compute(left_x)
    to_pair(left_x, 1)
    for group in range(chunks):
        arrived(rows.at[1 - core, right_x, slots(group)], pair_sems.at[2, group])
    compute(right_x)
    to_pair(right_x, 2)

    low, high = pl.ds(0, half_rows), pl.ds(half_rows, half_rows)
    pair_sum(left_x, 1)
    copies.start(chip_sum.at[left_x, low], ring_in.at[1, low], back_sems.at[4], seq, left)
    pair_sum(right_x, 2)
    copies.start(chip_sum.at[right_x, high], ring_in.at[0, high], back_sems.at[5], seq, right)

    for group in range(chunks):
        got = rows.at[core, far_x, slots(group)]
        arrived(got, ring_sems.at[2, group])
        copies.start(got, got, pair_sems.at[3, group], seq, partner)
    for group in range(chunks):
        arrived(rows.at[1 - core, far_x, slots(group)], pair_sems.at[3, group])
    compute(far_x)
    to_pair(far_x, 3)
    pair_sum(far_x, 3)
    copies.start(chip_sum.at[far_x, low], ring_opp.at[0], back_sems.at[6], seq, right)
    copies.start(chip_sum.at[far_x, high], ring_opp.at[1], back_sems.at[7], seq, left)
    pair_sum(x, 0)

    arrived(ring_opp.at[0], back_sems.at[6])
    chip_sum[right_x, low] = (
        chip_sum[right_x, low].astype(jnp.float32) + ring_opp[0].astype(jnp.float32)
    ).astype(jnp.bfloat16)
    copies.start(chip_sum.at[right_x, low], ring_in.at[0, low], back_sems.at[8], seq, right)
    arrived(ring_opp.at[1], back_sems.at[7])
    chip_sum[left_x, high] = (
        chip_sum[left_x, high].astype(jnp.float32) + ring_opp[1].astype(jnp.float32)
    ).astype(jnp.bfloat16)
    copies.start(chip_sum.at[left_x, high], ring_in.at[1, high], back_sems.at[9], seq, left)

    for part_rows, at, sems in ((low, 0, (8, 4)), (high, half_rows, (5, 9))):
        arrived(ring_in.at[0, part_rows], back_sems.at[sems[0]])
        arrived(ring_in.at[1, part_rows], back_sems.at[sems[1]])
        final[part_rows] = (
            chip_sum[x, part_rows].astype(jnp.float32)
            + ring_in[0, part_rows].astype(jnp.float32)
            + ring_in[1, part_rows].astype(jnp.float32)
        ).astype(jnp.bfloat16)
        for slot in range(at, at + half_rows):
            if slot:
                copies.start(
                    final.at[slot], returned.at[seq], back_sems.at[10 + slot], ahead(slot), tp
                )
    returned[seq] = final[0]
    for slot in range(1, n_seq):
        arrived(returned.at[behind(slot)], back_sems.at[10 + slot])
    terms = jnp.dot(
        picker[...],
        returned[...].reshape(n_seq * 8, width),
        preferred_element_type=jnp.float32,
    )
    count = mixed.shape[1]
    mixture = terms[: 2 * count] + terms[2 * count : 4 * count] + terms[4 * count :]
    mixed[...] = mixture.reshape(mixed.shape)
    copies.start(mixed.at[1 - core], mixed_in, attn_sems.at[5], seq, partner)
    arrived(mixed_in, attn_sems.at[5])
    out[...] = (residual[...] + (mixed[core] + mixed_in[...])).astype(jnp.bfloat16)
    copies.drain()


def moe(part, stream_rows, gain, placer, picker, w_gateup, w_down):
    n_seq = lax.axis_size("seq")
    n_x = lax.axis_size("tp") // 2
    count, width = stream_rows.shape
    hidden = w_down.shape[1]
    bf16, f32 = jnp.bfloat16, jnp.float32
    vmem, dma = pltpu.VMEM, pltpu.SemaphoreType.DMA
    chunks = n_seq // max(1, n_seq // 4)
    scratch = [
        vmem((n_x, count, width), bf16),
        vmem((n_x, count, width), bf16),
        vmem((3, count, width), bf16),
        vmem((count, width), f32),
        vmem((2, count, width), bf16),
        vmem((n_seq, 8, width), bf16),
        vmem((2, n_x, n_seq, 8, width), bf16),
        vmem((2, 2, hidden, width), bf16),
        vmem((2, hidden, width), bf16),
        vmem((2, n_x, n_seq, 8, width), bf16),
        vmem((n_x, n_seq, 8, width), bf16),
        vmem((n_x, n_seq, 8, width), bf16),
        vmem((2, n_seq // 2, 8, width), bf16),
        vmem((2, n_seq, 8, width), bf16),
        vmem((n_seq, 8, width), bf16),
        vmem((n_seq, 8, width), bf16),
        vmem((2, count, width), f32),
        vmem((count, width), f32),
        dma((2,)),
        dma((128,)),
        dma((6,)),
        dma((chunks,)),
        dma((3, chunks)),
        dma((4, chunks)),
        dma((10 + n_seq,)),
    ]
    in_vmem = pl.BlockSpec(memory_space=pltpu.VMEM)
    return pl.pallas_call(
        functools.partial(moe_kernel, n_seq, n_x),
        out_shape=jax.ShapeDtypeStruct((count, width), bf16),
        in_specs=[in_vmem] * 5 + [pl.BlockSpec(memory_space=pl.ANY)] * 2,
        out_specs=in_vmem,
        scratch_shapes=scratch,
        compiler_params=pltpu.CompilerParams(
            collective_id=0, has_side_effects=True, vmem_limit_bytes=60 * 1024 * 1024
        ),
    )(part, stream_rows, gain, placer, picker, w_gateup, w_down)


def routing(expert_index, gate_weight, seq_count, core):
    count = expert_index.shape[0]
    experts = 2 * seq_count
    own = jnp.concatenate([expert_index.astype(jnp.float32), gate_weight], axis=1)
    tp_count = lax.axis_size("tp")
    other = lax.ppermute(own, "tp", [(i, i ^ 1) for i in range(tp_count)])
    both = jnp.where(core == 0, jnp.stack([own, other]), jnp.stack([other, own]))
    holder = jnp.arange(seq_count, dtype=jnp.int32)
    named = both[:, :, :TOPK].astype(jnp.int32)[..., None] == (2 * holder + core)
    chosen = jnp.sum(named.astype(jnp.float32), axis=2)
    weight = jnp.sum(jnp.where(named, both[:, :, TOPK:, None], 0.0), axis=2)
    rank = jnp.cumsum(chosen, axis=1) - chosen
    place = jnp.arange(4, dtype=jnp.float32)
    hit = chosen[..., None] * (rank[..., None] == place)
    eye = jnp.eye(2, dtype=jnp.float32)
    hit = hit[:, :, :, None, :] * eye[:, None, None, :, None]
    picker = hit * weight[..., None, None]
    shape = (2 * count, seq_count * 8)
    placer = hit.reshape(shape).T.astype(jnp.bfloat16)
    picker = picker.reshape(shape)
    high = picker.astype(jnp.bfloat16)
    rest = picker - high.astype(jnp.float32)
    middle = rest.astype(jnp.bfloat16)
    low = (rest - middle.astype(jnp.float32)).astype(jnp.bfloat16)
    return placer, jnp.concatenate([high, middle, low], axis=0)


def local(
    stream_in,
    attn_gain,
    w_qkv,
    key_value_cache,
    w_out,
    mlp_gain,
    expert_index,
    gate_weight,
    w_gateup,
    w_down,
):
    seq_count = lax.axis_size("seq")
    tp_count = lax.axis_size("tp")
    tp = lax.axis_index("tp")
    length_local = stream_in.shape[0]
    heads_local = w_qkv.shape[1]
    query_group_width = QUERY_HEADS // KEY_VALUE_HEADS
    placer, picker = routing(expert_index, gate_weight, seq_count, tp % 2)
    normed = rms_scale(stream_in.astype(jnp.float32), attn_gain).astype(jnp.bfloat16)
    projected_rows = jnp.einsum(
        "td,dhc->thc", normed, w_qkv, preferred_element_type=jnp.float32
    ).astype(jnp.bfloat16)
    projected_rows = projected_rows.reshape(
        length_local, heads_local, query_group_width + 2, HEAD_SIZE
    )
    queries = projected_rows[:, :, :query_group_width]
    kv_tail_rows = jnp.concatenate(
        [
            projected_rows[length_local - WINDOW_KEYS :, :, query_group_width],
            projected_rows[length_local - WINDOW_KEYS :, :, query_group_width + 1],
        ],
        axis=-1,
    )
    earlier = from_behind(kv_tail_rows, "seq", 1)
    at_start = lax.axis_index("seq") == 0
    earlier = jnp.where(at_start, key_value_cache, earlier)
    key_rows = jnp.concatenate(
        [earlier[:, :, :HEAD_SIZE], projected_rows[:, :, query_group_width]], axis=0
    )
    value_rows = jnp.concatenate(
        [earlier[:, :, HEAD_SIZE:], projected_rows[:, :, query_group_width + 1]], axis=0
    )
    attended = window_block(queries, key_rows, value_rows).reshape(
        length_local, heads_local * query_group_width * HEAD_SIZE
    )
    block_rows = length_local // tp_count
    part = jnp.dot(attended, w_out, preferred_element_type=jnp.float32).astype(jnp.bfloat16)
    part = part.reshape(tp_count // 2, 2, block_rows, MODEL_WIDTH).transpose(1, 0, 2, 3)
    stream_rows = lax.dynamic_slice_in_dim(stream_in, tp * block_rows, block_rows, 0)
    return moe(
        part,
        stream_rows,
        mlp_gain[None],
        placer,
        picker,
        w_gateup.transpose(0, 2, 3, 1),
        w_down,
    )


def solution(mesh):
    in_specs = (
        P("seq", None),
        P(),
        P(None, "tp", None),
        P(None, "tp", None),
        P("tp", None),
        P(),
        P(("seq", "tp"), None),
        P(("seq", "tp"), None),
        P("seq", None, None, "tp"),
        P("seq", "tp", None),
    )
    out_specs = P(("seq", "tp"), None)
    return jax.shard_map(local, mesh=mesh, in_specs=in_specs, out_specs=out_specs, check_vma=False)
```

```python
import functools

import jax
import jax.numpy as jnp
from jax import lax
from jax.experimental import pallas as pl
from jax.experimental.pallas import tpu as pltpu
from jax.sharding import PartitionSpec as P

HEAD_SIZE = 64
WINDOW_KEYS = 128
TOPK = 4
EPS = 1e-05
MESH = pl.DeviceIdType.MESH
BF16, F32 = jnp.bfloat16, jnp.float32


def rms_scale(values, gain_vec):
    mean_sq = jnp.mean(values * values, axis=-1, keepdims=True)
    return values * lax.rsqrt(mean_sq + EPS) * gain_vec


def contract_last(a, b):
    return lax.dot_general(a, b, (((1,), (1,)), ((), ())), preferred_element_type=F32)


def contract_first(a, b):
    return lax.dot_general(a, b, (((0,), (0,)), ((), ())), preferred_element_type=F32)


class Copies:
    def __init__(self, send_sems):
        self.send_sems = send_sems
        self.started = []

    def start(self, src, dst, recv_sem, seq, tp):
        copy = pltpu.make_async_remote_copy(
            src_ref=src,
            dst_ref=dst,
            send_sem=self.send_sems.at[len(self.started)],
            recv_sem=recv_sem,
            device_id=(seq, tp),
            device_id_type=MESH,
        )
        copy.start()
        self.started.append(copy)

    def drain(self):
        for copy in self.started:
            copy.wait_send()


def arrived(ref, sem):
    pltpu.make_async_copy(ref, ref, sem).wait()


def window_attention(projected, earlier):
    length = projected.shape[0]
    pairs = projected.shape[1] // 128 - 1
    keyval = jnp.concatenate([earlier, projected[:, pairs * 128 :]], axis=0).astype(F32)
    swapped = pltpu.roll(keyval, 64, 1)
    low = lax.broadcasted_iota(jnp.int32, keyval.shape, 1) < HEAD_SIZE
    keys = [jnp.where(low, keyval, 0.0).astype(BF16), jnp.where(low, 0.0, swapped).astype(BF16)]
    values = [jnp.where(low, swapped, 0.0).astype(BF16), jnp.where(low, 0.0, keyval).astype(BF16)]
    queries = jnp.concatenate(
        [projected[:, pair * 128 : (pair + 1) * 128] for pair in range(pairs)], axis=0
    )
    shape = (queries.shape[0], keyval.shape[0])
    row = lax.broadcasted_iota(jnp.int32, shape, 0) % length
    offset = lax.broadcasted_iota(jnp.int32, shape, 1) - row
    in_window = (offset >= 1) & (offset <= WINDOW_KEYS)
    attended = None
    for side in range(2):
        scores = contract_last(queries, keys[side]) * HEAD_SIZE ** (-0.5)
        scores = jnp.where(in_window, scores, -1e30)
        exponent = jnp.exp(scores - jnp.max(scores, axis=-1, keepdims=True))
        weights = (exponent / jnp.sum(exponent, axis=-1, keepdims=True)).astype(BF16)
        term = jnp.dot(weights, values[side], preferred_element_type=F32)
        attended = term if attended is None else attended + term
    attended = attended.astype(BF16)
    return jnp.concatenate(
        [attended[pair * length : (pair + 1) * length] for pair in range(pairs)], axis=1
    )


def slot_table(route, core, n_seq, slot_core):
    count = route.shape[1]
    shape = (n_seq * 8, count)
    line = lax.broadcasted_iota(jnp.int32, shape, 0)
    expert = (line // 8 * 2 + core).astype(F32)
    chosen = jnp.zeros(shape, F32)
    weight = jnp.zeros(shape, F32)
    for k in range(TOPK):
        named = expert == route[k : k + 1, :]
        chosen = chosen + named.astype(F32)
        weight = weight + jnp.where(named, route[TOPK + k : TOPK + k + 1, :], 0.0)
    before = lax.broadcasted_iota(jnp.int32, (count, count), 0) < lax.broadcasted_iota(
        jnp.int32, (count, count), 1
    )
    rank = jnp.dot(chosen.astype(BF16), before.astype(BF16), preferred_element_type=F32)
    place = (line % 4).astype(F32)
    here = line % 8 // 4 == slot_core
    hit = jnp.where(here & (rank == place), chosen, 0.0)
    return hit.astype(BF16), hit * weight


def split3(values):
    high = values.astype(BF16)
    rest = values - high.astype(F32)
    middle = rest.astype(BF16)
    return high, middle, (rest - middle.astype(F32)).astype(BF16)


def layer_kernel(
    n_seq,
    n_x,
    route_own,
    attn_gain,
    mlp_gain,
    cache,
    stream_hbm,
    w_qkv_hbm,
    w_out_hbm,
    w_gateup_hbm,
    w_down_hbm,
    out,
    stream_t,
    w_qkv,
    w_out,
    tail,
    earlier,
    stream,
    route,
    part,
    attn_pair,
    attn_sum,
    attn_opp,
    attn_in,
    residual,
    hidden,
    packed,
    rows,
    w_gateup,
    w_down,
    product,
    from_pair,
    chip_sum,
    ring_opp,
    ring_in,
    final,
    returned,
    mixed,
    mixed_in,
    load_sems,
    send_sems,
    attn_sems,
    block_sems,
    ring_sems,
    pair_sems,
    back_sems,
    opp_sems,
    in_sems,
    home_sems,
):
    seq, tp = lax.axis_index("seq"), lax.axis_index("tp")
    x, core = tp // 2, tp % 2
    nz = 4 if n_seq % 4 == 0 else n_seq
    ny = n_seq // nz
    y, z = seq // nz, seq % nz
    partner = tp + 1 - 2 * core
    right_x, left_x, far_x = (x + 1) % n_x, (x + n_x - 1) % n_x, (x + 2) % n_x
    right, left, far = right_x * 2 + core, left_x * 2 + core, far_x * 2 + core
    chunk = max(1, n_seq // 4)
    chunks = n_seq // chunk
    half = chunks // 2
    y_steps = [0, 2, 1, 3] if ny == 4 else list(range(ny))
    first_order = [0, 2, 3, 1] if chunks == 4 else list(range(chunks))
    low_order = list(range(half))[::-1]
    high_order = list(range(half, chunks))
    width = out.shape[-1]
    length = stream.shape[0] * stream.shape[1]
    copies = Copies(send_sems)

    def load(src, dst, index):
        copy = pltpu.make_async_copy(src, dst, load_sems.at[index])
        copy.start()
        return copy

    edges = [0, width // 3 // 128 * 128, width * 2 // 3 // 128 * 128, width]
    spans = [pl.ds(a, b - a) for a, b in zip(edges[:-1], edges[1:]) if b > a]
    stream_load = load(stream_hbm, stream_t, 0)
    qkv_loads = [
        load(w_qkv_hbm.at[span], w_qkv.at[span], 1 + i) for i, span in enumerate(spans)
    ]
    out_load = load(w_out_hbm, w_out, 4)

    def behind(slot):
        dy, dz = y_steps[slot // nz], slot % nz
        return ((y + ny - dy) % ny) * nz + (z + nz - dz) % nz

    def ahead(slot):
        dy, dz = y_steps[slot // nz], slot % nz
        return ((y + dy) % ny) * nz + (z + dz) % nz

    barrier = pltpu.get_barrier_semaphore()
    after = (seq + 1) % n_seq
    for slot in range(1, n_seq):
        pl.semaphore_signal(barrier, inc=1, device_id=(ahead(slot), tp), device_id_type=MESH)
    for peer in (partner, right, left):
        pl.semaphore_signal(barrier, inc=1, device_id=(seq, peer), device_id_type=MESH)
    route[core] = route_own[...]

    square = lax.broadcasted_iota(jnp.int32, (length, length), 0)
    eye = (square == lax.broadcasted_iota(jnp.int32, (length, length), 1)).astype(BF16)
    stream_load.wait()
    tokens = contract_last(eye, stream_t[...])
    stream[...] = tokens.astype(BF16).reshape(stream.shape)
    normed = rms_scale(tokens, attn_gain[...]).astype(BF16)
    projected = None
    for span, (a, b), copy in zip(spans, zip(edges[:-1], edges[1:]), qkv_loads):
        copy.wait()
        term = jnp.dot(normed[:, a:b], w_qkv[span], preferred_element_type=F32)
        projected = term if projected is None else projected + term
    projected = projected.astype(BF16)
    tail[...] = projected[:, projected.shape[1] - 128 :]
    pl.semaphore_wait(barrier, n_seq - 1 + 3)
    copies.start(tail, earlier, attn_sems.at[0], after, tp)
    copies.start(route.at[core], route.at[core], attn_sems.at[1], seq, partner)
    arrived(earlier, attn_sems.at[0])
    attended = window_attention(projected, jnp.where(seq == 0, cache[...], earlier[...]))
    out_load.wait()
    weight_loads = [load(w_gateup_hbm, w_gateup, 5), load(w_down_hbm, w_down, 6)]
    part[...] = contract_last(attended, w_out[...]).reshape(part.shape).astype(BF16)

    copies.start(part.at[:, 1 - core], attn_pair, attn_sems.at[2], seq, partner)
    arrived(route.at[1 - core], attn_sems.at[1])
    tables = [slot_table(route[c], core, n_seq, c) for c in range(2)]
    arrived(attn_pair, attn_sems.at[2])

    def pair_total(peer_x):
        return part[peer_x, core].astype(F32) + attn_pair[peer_x].astype(F32)

    attn_sum[far_x] = pair_total(far_x).astype(BF16)
    copies.start(attn_sum.at[far_x, 0], attn_opp.at[0], attn_sems.at[3], seq, right)
    copies.start(attn_sum.at[far_x, 1], attn_opp.at[1], attn_sems.at[4], seq, left)
    attn_sum[right_x] = pair_total(right_x).astype(BF16)
    copies.start(attn_sum.at[right_x, 1], attn_in.at[0, 1], attn_sems.at[5], seq, right)
    attn_sum[left_x] = pair_total(left_x).astype(BF16)
    copies.start(attn_sum.at[left_x, 0], attn_in.at[1, 0], attn_sems.at[6], seq, left)
    total = stream[tp].astype(F32).reshape(2, -1, width) + pair_total(x)
    arrived(attn_opp.at[0], attn_sems.at[3])
    attn_sum[right_x, 0] = (
        attn_sum[right_x, 0].astype(F32) + attn_opp[0].astype(F32)
    ).astype(BF16)
    copies.start(attn_sum.at[right_x, 0], attn_in.at[0, 0], attn_sems.at[7], seq, right)
    arrived(attn_opp.at[1], attn_sems.at[4])
    attn_sum[left_x, 1] = (
        attn_sum[left_x, 1].astype(F32) + attn_opp[1].astype(F32)
    ).astype(BF16)
    copies.start(attn_sum.at[left_x, 1], attn_in.at[1, 1], attn_sems.at[8], seq, left)
    for which, part_of, sem in ((0, 1, 5), (1, 0, 6), (0, 0, 7), (1, 1, 8)):
        arrived(attn_in.at[which, part_of], attn_sems.at[sem])
    total = (total + attn_in[0].astype(F32) + attn_in[1].astype(F32)).reshape(-1, width)
    residual[...] = total
    hidden[core] = rms_scale(total, mlp_gain[...]).astype(BF16)
    copies.start(hidden.at[core], hidden.at[core], attn_sems.at[9], seq, partner)
    arrived(hidden.at[1 - core], attn_sems.at[9])

    packed[...] = (
        (
            jnp.dot(tables[0][0], hidden[0], preferred_element_type=F32)
            + jnp.dot(tables[1][0], hidden[1], preferred_element_type=F32)
        )
        .reshape(packed.shape)
        .astype(BF16)
    )
    for group in first_order:
        for slot in range(group * chunk, (group + 1) * chunk):
            if slot:
                copies.start(
                    packed.at[behind(slot)],
                    rows.at[core, x, slot],
                    block_sems.at[group],
                    behind(slot),
                    tp,
                )
    rows[core, x, 0] = packed[seq]

    def slots(group):
        return pl.ds(group * chunk, chunk)

    def spread(group):
        first = 1 if group == 0 else 0
        if chunk > first:
            got = rows.at[core, x, pl.ds(group * chunk + first, chunk - first)]
            arrived(got, block_sems.at[group])
        own = rows.at[core, x, slots(group)]
        copies.start(own, own, ring_sems.at[0, group], seq, right)
        copies.start(own, own, ring_sems.at[1, group], seq, left)
        copies.start(own, own, pair_sems.at[0, group], seq, partner)

    done = set()

    def take(from_left, group):
        if (from_left, group) in done:
            return
        done.add((from_left, group))
        got = rows.at[core, left_x if from_left else right_x, slots(group)]
        arrived(got, ring_sems.at[0 if from_left else 1, group])
        if from_left and group < half:
            copies.start(got, got, ring_sems.at[2, group], seq, right)
        if not from_left and group >= half:
            copies.start(got, got, ring_sems.at[2, group], seq, left)
        copies.start(got, got, pair_sems.at[1 if from_left else 2, group], seq, partner)

    def compute(block_x, which, expert):
        taken = rows[expert, block_x].reshape(n_seq * 8, width)
        gate = contract_last(taken, w_gateup[expert, 0])
        up = contract_last(taken, w_gateup[expert, 1])
        activated = (gate / (1.0 + jnp.exp(-gate)) * up).astype(BF16)
        result = jnp.dot(activated, w_down[expert], preferred_element_type=F32)
        product[expert, block_x] = result.reshape(n_seq, 8, width).astype(BF16)

    def block(block_x, which):
        for group in range(chunks):
            arrived(rows.at[1 - core, block_x, slots(group)], pair_sems.at[which, group])
        compute(block_x, which, 1 - core)
        for group in range(chunks):
            copies.start(
                product.at[1 - core, block_x, slots(group)],
                from_pair.at[block_x, slots(group)],
                back_sems.at[which, group],
                seq,
                partner,
            )
        compute(block_x, which, core)

    def pair_sum(block_x, which, group):
        at = slots(group)
        arrived(from_pair.at[block_x, at], back_sems.at[which, group])
        chip_sum[block_x, at] = (
            product[core, block_x, at].astype(F32) + from_pair[block_x, at].astype(F32)
        ).astype(BF16)

    for group in first_order[:-1]:
        spread(group)
    take(True, 0)
    if half in first_order[:-1]:
        take(False, half)
    spread(first_order[-1])
    take(False, chunks - 1)
    for copy in weight_loads:
        copy.wait()
    block(x, 0)
    for group in range(chunks):
        take(True, first_order[group])
        take(False, first_order[group])
    block(left_x, 1)
    block(right_x, 2)
    for group in high_order:
        pair_sum(right_x, 2, group)
        copies.start(
            chip_sum.at[right_x, slots(group)],
            ring_in.at[0, slots(group)],
            in_sems.at[0, group],
            seq,
            right,
        )
    for group in low_order:
        pair_sum(left_x, 1, group)
        copies.start(
            chip_sum.at[left_x, slots(group)],
            ring_in.at[1, slots(group)],
            in_sems.at[1, group],
            seq,
            left,
        )

    for group in range(chunks):
        got = rows.at[core, far_x, slots(group)]
        arrived(got, ring_sems.at[2, group])
        copies.start(got, got, pair_sems.at[3, group], seq, partner)
    block(far_x, 3)
    for low, high in zip(low_order, high_order):
        pair_sum(far_x, 3, low)
        copies.start(
            chip_sum.at[far_x, slots(low)], ring_opp.at[slots(low)], opp_sems.at[low], seq, right
        )
        pair_sum(far_x, 3, high)
        copies.start(
            chip_sum.at[far_x, slots(high)], ring_opp.at[slots(high)], opp_sems.at[high], seq, left
        )
    for low, high in zip(low_order, high_order):
        pair_sum(right_x, 2, low)
        pair_sum(left_x, 1, high)
        pair_sum(x, 0, low)
        pair_sum(x, 0, high)
    for low, high in zip(low_order, high_order):
        for group, peer_x, peer, side in ((low, right_x, right, 0), (high, left_x, left, 1)):
            at = slots(group)
            arrived(ring_opp.at[at], opp_sems.at[group])
            chip_sum[peer_x, at] = (
                chip_sum[peer_x, at].astype(F32) + ring_opp[at].astype(F32)
            ).astype(BF16)
            copies.start(
                chip_sum.at[peer_x, at], ring_in.at[side, at], in_sems.at[side, group], seq, peer
            )

    for low, high in zip(low_order, high_order):
        for group in (low, high):
            at = slots(group)
            arrived(ring_in.at[0, at], in_sems.at[0, group])
            arrived(ring_in.at[1, at], in_sems.at[1, group])
            final[at] = (
                chip_sum[x, at].astype(F32)
                + ring_in[0, at].astype(F32)
                + ring_in[1, at].astype(F32)
            ).astype(BF16)
            for slot in range(group * chunk, (group + 1) * chunk):
                if slot:
                    copies.start(
                        final.at[slot], returned.at[seq], home_sems.at[slot], ahead(slot), tp
                    )
    returned[seq] = final[0]
    pickers = [split3(table[1]) for table in tables]
    for slot in range(1, n_seq):
        arrived(returned.at[behind(slot)], home_sems.at[slot])
    terms = returned[...].reshape(n_seq * 8, width)
    for c in range(2):
        mixed[c] = sum(contract_first(piece, terms) for piece in pickers[c])
    copies.start(mixed.at[1 - core], mixed_in, attn_sems.at[10], seq, partner)
    arrived(mixed_in, attn_sems.at[10])
    out[...] = (residual[...] + (mixed[core] + mixed_in[...])).astype(BF16)
    copies.drain()


def local(
    stream_in,
    attn_gain,
    w_qkv,
    key_value_cache,
    w_out,
    mlp_gain,
    expert_index,
    gate_weight,
    w_gateup,
    w_down,
):
    n_seq = lax.axis_size("seq")
    n_tp = lax.axis_size("tp")
    n_x = n_tp // 2
    length, width = stream_in.shape
    count = length // n_tp
    hidden = w_down.shape[1]
    columns = w_qkv.shape[2]
    heads_width = w_out.shape[0]
    route = jnp.concatenate([expert_index.astype(F32), gate_weight], axis=1).T
    vmem, dma = pltpu.VMEM, pltpu.SemaphoreType.DMA
    chunks = n_seq // max(1, n_seq // 4)
    scratch = [
        vmem((width, length), BF16),
        vmem((width, columns), BF16),
        vmem((width, heads_width), BF16),
        vmem((length, 128), BF16),
        vmem((length, 128), BF16),
        vmem((n_tp, count, width), BF16),
        vmem((2, 2 * TOPK, count), F32),
        vmem((n_x, 2, 2, count // 2, width), BF16),
        vmem((n_x, 2, count // 2, width), BF16),
        vmem((n_x, 2, count // 2, width), BF16),
        vmem((2, count // 2, width), BF16),
        vmem((2, 2, count // 2, width), BF16),
        vmem((count, width), F32),
        vmem((2, count, width), BF16),
        vmem((n_seq, 8, width), BF16),
        vmem((2, n_x, n_seq, 8, width), BF16),
        vmem((2, 2, hidden, width), BF16),
        vmem((2, hidden, width), BF16),
        vmem((2, n_x, n_seq, 8, width), BF16),
        vmem((n_x, n_seq, 8, width), BF16),
        vmem((n_x, n_seq, 8, width), BF16),
        vmem((n_seq, 8, width), BF16),
        vmem((2, n_seq, 8, width), BF16),
        vmem((n_seq, 8, width), BF16),
        vmem((n_seq, 8, width), BF16),
        vmem((2, count, width), F32),
        vmem((count, width), F32),
        dma((7,)),
        dma((160,)),
        dma((11,)),
        dma((chunks,)),
        dma((3, chunks)),
        dma((4, chunks)),
        dma((4, chunks)),
        dma((chunks,)),
        dma((2, chunks)),
        dma((n_seq,)),
    ]
    in_vmem = pl.BlockSpec(memory_space=pltpu.VMEM)
    return pl.pallas_call(
        functools.partial(layer_kernel, n_seq, n_x),
        out_shape=jax.ShapeDtypeStruct((count, width), BF16),
        in_specs=[in_vmem] * 4 + [pl.BlockSpec(memory_space=pl.ANY)] * 5,
        out_specs=in_vmem,
        scratch_shapes=scratch,
        compiler_params=pltpu.CompilerParams(
            collective_id=0, has_side_effects=True, vmem_limit_bytes=63 * 1024 * 1024
        ),
    )(
        route,
        attn_gain[None],
        mlp_gain[None],
        key_value_cache.reshape(length, 128),
        stream_in.T,
        w_qkv.reshape(width, columns),
        w_out.T,
        w_gateup.transpose(0, 2, 3, 1),
        w_down,
    )


def solution(mesh):
    in_specs = (
        P("seq", None),
        P(),
        P(None, "tp", None),
        P(None, "tp", None),
        P("tp", None),
        P(),
        P(("seq", "tp"), None),
        P(("seq", "tp"), None),
        P("seq", None, None, "tp"),
        P("seq", "tp", None),
    )
    out_specs = P(("seq", "tp"), None)
    return jax.shard_map(local, mesh=mesh, in_specs=in_specs, out_specs=out_specs, check_vma=False)
```

```python
import functools

import jax
import jax.numpy as jnp
from jax import lax
from jax.experimental import pallas as pl
from jax.experimental.pallas import tpu as pltpu
from jax.sharding import PartitionSpec as P

HEAD_SIZE = 64
WINDOW_KEYS = 128
TOPK = 4
EPS = 1e-05
MESH = pl.DeviceIdType.MESH
BF16, F32 = jnp.bfloat16, jnp.float32


def rms_scale(values, gain_vec):
    mean_sq = jnp.mean(values * values, axis=-1, keepdims=True)
    return values * lax.rsqrt(mean_sq + EPS) * gain_vec


def contract_last(a, b):
    return lax.dot_general(a, b, (((1,), (1,)), ((), ())), preferred_element_type=F32)


def contract_first(a, b):
    return lax.dot_general(a, b, (((0,), (0,)), ((), ())), preferred_element_type=F32)


class Copies:
    def __init__(self, send_sems):
        self.send_sems = send_sems
        self.started = []

    def start(self, src, dst, recv_sem, seq, tp):
        copy = pltpu.make_async_remote_copy(
            src_ref=src,
            dst_ref=dst,
            send_sem=self.send_sems.at[len(self.started)],
            recv_sem=recv_sem,
            device_id=(seq, tp),
            device_id_type=MESH,
        )
        copy.start()
        self.started.append(copy)

    def drain(self):
        for copy in self.started:
            copy.wait_send()


def arrived(ref, sem):
    pltpu.make_async_copy(ref, ref, sem).wait()


def key_value_sides(keyval):
    keyval = keyval.astype(F32)
    swapped = pltpu.roll(keyval, 64, 1)
    low = lax.broadcasted_iota(jnp.int32, keyval.shape, 1) < HEAD_SIZE
    keys = [jnp.where(low, keyval, 0.0).astype(BF16), jnp.where(low, 0.0, swapped).astype(BF16)]
    values = [jnp.where(low, swapped, 0.0).astype(BF16), jnp.where(low, 0.0, keyval).astype(BF16)]
    return keys, values


def own_scores(projected):
    length = projected.shape[0]
    pairs = projected.shape[1] // 128 - 1
    keys, values = key_value_sides(projected[:, pairs * 128 :])
    queries = jnp.concatenate(
        [projected[:, pair * 128 : (pair + 1) * 128] for pair in range(pairs)], axis=0
    )
    shape = (queries.shape[0], length)
    row = lax.broadcasted_iota(jnp.int32, shape, 0) % length
    later = lax.broadcasted_iota(jnp.int32, shape, 1) > row
    scores = [
        jnp.where(later, -1e30, contract_last(queries, key) * HEAD_SIZE ** (-0.5)) for key in keys
    ]
    return queries, later, scores, values


def window_attention(prepared, earlier):
    queries, later, own, own_values = prepared
    keys, values = key_value_sides(earlier)
    attended = None
    for side in range(2):
        before = contract_last(queries, keys[side]) * HEAD_SIZE ** (-0.5)
        scores = jnp.concatenate([jnp.where(later, before, -1e30), own[side]], axis=1)
        exponent = jnp.exp(scores - jnp.max(scores, axis=-1, keepdims=True))
        weights = (exponent / jnp.sum(exponent, axis=-1, keepdims=True)).astype(BF16)
        both = jnp.concatenate([values[side], own_values[side]], axis=0)
        term = jnp.dot(weights, both, preferred_element_type=F32)
        attended = term if attended is None else attended + term
    attended = attended.astype(BF16)
    length = earlier.shape[0]
    return jnp.concatenate(
        [attended[at : at + length] for at in range(0, attended.shape[0], length)], axis=1
    )


def slot_table(route, core, n_seq, slot_core):
    count = route.shape[1]
    shape = (n_seq * 8, count)
    line = lax.broadcasted_iota(jnp.int32, shape, 0)
    expert = (line // 8 * 2 + core).astype(F32)
    chosen = jnp.zeros(shape, F32)
    weight = jnp.zeros(shape, F32)
    for k in range(TOPK):
        named = expert == route[k : k + 1, :]
        chosen = chosen + named.astype(F32)
        weight = weight + jnp.where(named, route[TOPK + k : TOPK + k + 1, :], 0.0)
    before = lax.broadcasted_iota(jnp.int32, (count, count), 0) < lax.broadcasted_iota(
        jnp.int32, (count, count), 1
    )
    rank = jnp.dot(chosen.astype(BF16), before.astype(BF16), preferred_element_type=F32)
    place = (line % 4).astype(F32)
    here = line % 8 // 4 == slot_core
    hit = jnp.where(here & (rank == place), chosen, 0.0)
    return hit.astype(BF16), hit * weight


def split3(values):
    high = values.astype(BF16)
    rest = values - high.astype(F32)
    middle = rest.astype(BF16)
    return high, middle, (rest - middle.astype(F32)).astype(BF16)


def layer_kernel(
    n_seq,
    n_x,
    index_own,
    weight_own,
    attn_gain,
    mlp_gain,
    cache,
    stream_hbm,
    w_qkv_hbm,
    w_out_hbm,
    w_gateup_hbm,
    w_down_hbm,
    out,
    stream_t,
    w_qkv,
    w_out,
    tail,
    earlier,
    stream,
    route,
    part,
    attn_pair,
    attn_sum,
    attn_opp,
    attn_in,
    residual,
    hidden,
    packed,
    rows,
    w_gateup,
    w_down,
    product,
    from_pair,
    chip_sum,
    ring_opp,
    ring_in,
    final,
    returned,
    mixed,
    mixed_in,
    load_sems,
    send_sems,
    attn_sems,
    block_sems,
    ring_sems,
    pair_sems,
    back_sems,
    opp_sems,
    in_sems,
    home_sems,
):
    seq, tp = lax.axis_index("seq"), lax.axis_index("tp")
    x, core = tp // 2, tp % 2
    nz = 4 if n_seq % 4 == 0 else n_seq
    ny = n_seq // nz
    y, z = seq // nz, seq % nz
    partner = tp + 1 - 2 * core
    right_x, left_x, far_x = (x + 1) % n_x, (x + n_x - 1) % n_x, (x + 2) % n_x
    right, left, far = right_x * 2 + core, left_x * 2 + core, far_x * 2 + core
    chunk = max(1, n_seq // 4)
    chunks = n_seq // chunk
    half = chunks // 2
    y_steps = [0, 2, 1, 3] if ny == 4 else list(range(ny))
    first_order = [0, 2, 3, 1] if chunks == 4 else list(range(chunks))
    low_order = list(range(half))[::-1]
    high_order = list(range(half, chunks))
    width = out.shape[-1]
    length = stream.shape[0] * stream.shape[1]
    copies = Copies(send_sems)

    def load(src, dst, index):
        copy = pltpu.make_async_copy(src, dst, load_sems.at[index])
        copy.start()
        return copy

    edges = [0, width // 3 // 128 * 128, width * 2 // 3 // 128 * 128, width]
    spans = [pl.ds(a, b - a) for a, b in zip(edges[:-1], edges[1:]) if b > a]
    stream_load = load(stream_hbm, stream_t, 0)
    qkv_loads = [
        load(w_qkv_hbm.at[span], w_qkv.at[span], 1 + i) for i, span in enumerate(spans)
    ]
    out_load = load(w_out_hbm, w_out, 4)

    def behind(slot):
        dy, dz = y_steps[slot // nz], slot % nz
        return ((y + ny - dy) % ny) * nz + (z + nz - dz) % nz

    def ahead(slot):
        dy, dz = y_steps[slot // nz], slot % nz
        return ((y + dy) % ny) * nz + (z + dz) % nz

    barrier = pltpu.get_barrier_semaphore()
    after = (seq + 1) % n_seq
    for slot in range(1, n_seq):
        pl.semaphore_signal(barrier, inc=1, device_id=(ahead(slot), tp), device_id_type=MESH)
    for peer in (partner, right, left):
        pl.semaphore_signal(barrier, inc=1, device_id=(seq, peer), device_id_type=MESH)
    route[core, 0:TOPK] = index_own[...].astype(F32)
    route[core, TOPK:] = weight_own[...]

    square = lax.broadcasted_iota(jnp.int32, (length, length), 0)
    eye = (square == lax.broadcasted_iota(jnp.int32, (length, length), 1)).astype(BF16)
    stream_load.wait()
    tokens = contract_last(eye, stream_t[...])
    stream[...] = tokens.astype(BF16).reshape(stream.shape)
    normed = rms_scale(tokens, attn_gain[...].reshape(1, -1)).astype(BF16)
    projected = None
    for span, (a, b), copy in zip(spans, zip(edges[:-1], edges[1:]), qkv_loads):
        copy.wait()
        term = jnp.dot(normed[:, a:b], w_qkv[span], preferred_element_type=F32)
        projected = term if projected is None else projected + term
    projected = projected.astype(BF16)
    tail[...] = projected[:, projected.shape[1] - 128 :]
    pl.semaphore_wait(barrier, n_seq - 1 + 3)
    copies.start(tail, earlier, attn_sems.at[0], after, tp)
    copies.start(route.at[core], route.at[core], attn_sems.at[1], seq, partner)
    prepared = own_scores(projected)
    arrived(earlier, attn_sems.at[0])
    attended = window_attention(prepared, jnp.where(seq == 0, cache[...], earlier[...]))
    out_load.wait()
    weight_loads = [load(w_gateup_hbm, w_gateup, 5), load(w_down_hbm, w_down, 6)]
    part[...] = contract_last(attended, w_out[...]).reshape(part.shape).astype(BF16)

    copies.start(part.at[:, 1 - core], attn_pair, attn_sems.at[2], seq, partner)
    arrived(route.at[1 - core], attn_sems.at[1])
    tables = [slot_table(route[c], core, n_seq, c) for c in range(2)]
    arrived(attn_pair, attn_sems.at[2])

    def pair_total(peer_x):
        return part[peer_x, core].astype(F32) + attn_pair[peer_x].astype(F32)

    attn_sum[far_x] = pair_total(far_x).astype(BF16)
    copies.start(attn_sum.at[far_x, 0], attn_opp.at[0], attn_sems.at[3], seq, right)
    copies.start(attn_sum.at[far_x, 1], attn_opp.at[1], attn_sems.at[4], seq, left)
    attn_sum[right_x] = pair_total(right_x).astype(BF16)
    copies.start(attn_sum.at[right_x, 1], attn_in.at[0, 1], attn_sems.at[5], seq, right)
    attn_sum[left_x] = pair_total(left_x).astype(BF16)
    copies.start(attn_sum.at[left_x, 0], attn_in.at[1, 0], attn_sems.at[6], seq, left)
    total = stream[tp].astype(F32).reshape(2, -1, width) + pair_total(x)
    arrived(attn_opp.at[0], attn_sems.at[3])
    attn_sum[right_x, 0] = (
        attn_sum[right_x, 0].astype(F32) + attn_opp[0].astype(F32)
    ).astype(BF16)
    copies.start(attn_sum.at[right_x, 0], attn_in.at[0, 0], attn_sems.at[7], seq, right)
    arrived(attn_opp.at[1], attn_sems.at[4])
    attn_sum[left_x, 1] = (
        attn_sum[left_x, 1].astype(F32) + attn_opp[1].astype(F32)
    ).astype(BF16)
    copies.start(attn_sum.at[left_x, 1], attn_in.at[1, 1], attn_sems.at[8], seq, left)
    for which, part_of, sem in ((0, 1, 5), (1, 0, 6), (0, 0, 7), (1, 1, 8)):
        arrived(attn_in.at[which, part_of], attn_sems.at[sem])
    total = (total + attn_in[0].astype(F32) + attn_in[1].astype(F32)).reshape(-1, width)
    residual[...] = total
    hidden[core] = rms_scale(total, mlp_gain[...].reshape(1, -1)).astype(BF16)
    copies.start(hidden.at[core], hidden.at[core], attn_sems.at[9], seq, partner)
    arrived(hidden.at[1 - core], attn_sems.at[9])

    packed[...] = (
        (
            jnp.dot(tables[0][0], hidden[0], preferred_element_type=F32)
            + jnp.dot(tables[1][0], hidden[1], preferred_element_type=F32)
        )
        .reshape(packed.shape)
        .astype(BF16)
    )
    for group in first_order:
        for slot in range(group * chunk, (group + 1) * chunk):
            if slot:
                copies.start(
                    packed.at[behind(slot)],
                    rows.at[core, x, slot],
                    block_sems.at[group],
                    behind(slot),
                    tp,
                )
    rows[core, x, 0] = packed[seq]

    def slots(group):
        return pl.ds(group * chunk, chunk)

    def spread(group):
        first = 1 if group == 0 else 0
        if chunk > first:
            got = rows.at[core, x, pl.ds(group * chunk + first, chunk - first)]
            arrived(got, block_sems.at[group])
        own = rows.at[core, x, slots(group)]
        copies.start(own, own, ring_sems.at[0, group], seq, right)
        copies.start(own, own, ring_sems.at[1, group], seq, left)
        copies.start(own, own, pair_sems.at[0, group], seq, partner)

    done = set()

    def take(from_left, group):
        if (from_left, group) in done:
            return
        done.add((from_left, group))
        got = rows.at[core, left_x if from_left else right_x, slots(group)]
        arrived(got, ring_sems.at[0 if from_left else 1, group])
        if from_left and group < half:
            copies.start(got, got, ring_sems.at[2, group], seq, right)
        if not from_left and group >= half:
            copies.start(got, got, ring_sems.at[2, group], seq, left)
        copies.start(got, got, pair_sems.at[1 if from_left else 2, group], seq, partner)

    def compute(block_x, which, expert):
        taken = rows[expert, block_x].reshape(n_seq * 8, width)
        gate = contract_last(taken, w_gateup[expert, 0])
        up = contract_last(taken, w_gateup[expert, 1])
        activated = (gate / (1.0 + jnp.exp(-gate)) * up).astype(BF16)
        result = jnp.dot(activated, w_down[expert], preferred_element_type=F32)
        product[expert, block_x] = result.reshape(n_seq, 8, width).astype(BF16)

    def block(block_x, which):
        for group in range(chunks):
            arrived(rows.at[1 - core, block_x, slots(group)], pair_sems.at[which, group])
        compute(block_x, which, 1 - core)
        for group in range(chunks):
            copies.start(
                product.at[1 - core, block_x, slots(group)],
                from_pair.at[block_x, slots(group)],
                back_sems.at[which, group],
                seq,
                partner,
            )
        compute(block_x, which, core)

    def pair_sum(block_x, which, group):
        at = slots(group)
        arrived(from_pair.at[block_x, at], back_sems.at[which, group])
        chip_sum[block_x, at] = (
            product[core, block_x, at].astype(F32) + from_pair[block_x, at].astype(F32)
        ).astype(BF16)

    for group in first_order[:-1]:
        spread(group)
    take(True, 0)
    if half in first_order[:-1]:
        take(False, half)
    spread(first_order[-1])
    take(False, chunks - 1)
    for copy in weight_loads:
        copy.wait()
    block(x, 0)
    for group in range(chunks):
        take(True, first_order[group])
        take(False, first_order[group])
    block(left_x, 1)
    block(right_x, 2)
    for group in high_order:
        pair_sum(right_x, 2, group)
        copies.start(
            chip_sum.at[right_x, slots(group)],
            ring_in.at[0, slots(group)],
            in_sems.at[0, group],
            seq,
            right,
        )
    for group in low_order:
        pair_sum(left_x, 1, group)
        copies.start(
            chip_sum.at[left_x, slots(group)],
            ring_in.at[1, slots(group)],
            in_sems.at[1, group],
            seq,
            left,
        )

    for group in range(chunks):
        got = rows.at[core, far_x, slots(group)]
        arrived(got, ring_sems.at[2, group])
        copies.start(got, got, pair_sems.at[3, group], seq, partner)
    block(far_x, 3)
    for low, high in zip(low_order, high_order):
        pair_sum(far_x, 3, low)
        copies.start(
            chip_sum.at[far_x, slots(low)], ring_opp.at[slots(low)], opp_sems.at[low], seq, right
        )
        pair_sum(far_x, 3, high)
        copies.start(
            chip_sum.at[far_x, slots(high)], ring_opp.at[slots(high)], opp_sems.at[high], seq, left
        )
    for low, high in zip(low_order, high_order):
        pair_sum(right_x, 2, low)
        pair_sum(left_x, 1, high)
        pair_sum(x, 0, low)
        pair_sum(x, 0, high)
    for low, high in zip(low_order, high_order):
        for group, peer_x, peer, side in ((low, right_x, right, 0), (high, left_x, left, 1)):
            at = slots(group)
            arrived(ring_opp.at[at], opp_sems.at[group])
            chip_sum[peer_x, at] = (
                chip_sum[peer_x, at].astype(F32) + ring_opp[at].astype(F32)
            ).astype(BF16)
            copies.start(
                chip_sum.at[peer_x, at], ring_in.at[side, at], in_sems.at[side, group], seq, peer
            )

    for low, high in zip(low_order, high_order):
        for group in (low, high):
            at = slots(group)
            arrived(ring_in.at[0, at], in_sems.at[0, group])
            arrived(ring_in.at[1, at], in_sems.at[1, group])
            final[at] = (
                chip_sum[x, at].astype(F32)
                + ring_in[0, at].astype(F32)
                + ring_in[1, at].astype(F32)
            ).astype(BF16)
            for slot in range(group * chunk, (group + 1) * chunk):
                if slot:
                    copies.start(
                        final.at[slot], returned.at[seq], home_sems.at[slot], ahead(slot), tp
                    )
    returned[seq] = final[0]
    pickers = [split3(table[1]) for table in tables]
    for slot in range(1, n_seq):
        arrived(returned.at[behind(slot)], home_sems.at[slot])
    terms = returned[...].reshape(n_seq * 8, width)
    for c in range(2):
        mixed[c] = sum(contract_first(piece, terms) for piece in pickers[c])
    copies.start(mixed.at[1 - core], mixed_in, attn_sems.at[10], seq, partner)
    arrived(mixed_in, attn_sems.at[10])
    out[...] = (residual[...] + (mixed[core] + mixed_in[...])).astype(BF16)
    copies.drain()


def local(
    stream_in,
    attn_gain,
    w_qkv,
    key_value_cache,
    w_out,
    mlp_gain,
    expert_index,
    gate_weight,
    w_gateup,
    w_down,
):
    n_seq = lax.axis_size("seq")
    n_tp = lax.axis_size("tp")
    n_x = n_tp // 2
    length, width = stream_in.shape
    count = length // n_tp
    hidden = w_down.shape[1]
    columns = w_qkv.shape[2]
    heads_width = w_out.shape[0]
    vmem, dma = pltpu.VMEM, pltpu.SemaphoreType.DMA
    chunks = n_seq // max(1, n_seq // 4)
    scratch = [
        vmem((width, length), BF16),
        vmem((width, columns), BF16),
        vmem((width, heads_width), BF16),
        vmem((length, 128), BF16),
        vmem((length, 128), BF16),
        vmem((n_tp, count, width), BF16),
        vmem((2, 2 * TOPK, count), F32),
        vmem((n_x, 2, 2, count // 2, width), BF16),
        vmem((n_x, 2, count // 2, width), BF16),
        vmem((n_x, 2, count // 2, width), BF16),
        vmem((2, count // 2, width), BF16),
        vmem((2, 2, count // 2, width), BF16),
        vmem((count, width), F32),
        vmem((2, count, width), BF16),
        vmem((n_seq, 8, width), BF16),
        vmem((2, n_x, n_seq, 8, width), BF16),
        vmem((2, 2, hidden, width), BF16),
        vmem((2, hidden, width), BF16),
        vmem((2, n_x, n_seq, 8, width), BF16),
        vmem((n_x, n_seq, 8, width), BF16),
        vmem((n_x, n_seq, 8, width), BF16),
        vmem((n_seq, 8, width), BF16),
        vmem((2, n_seq, 8, width), BF16),
        vmem((n_seq, 8, width), BF16),
        vmem((n_seq, 8, width), BF16),
        vmem((2, count, width), F32),
        vmem((count, width), F32),
        dma((7,)),
        dma((160,)),
        dma((11,)),
        dma((chunks,)),
        dma((3, chunks)),
        dma((4, chunks)),
        dma((4, chunks)),
        dma((chunks,)),
        dma((2, chunks)),
        dma((n_seq,)),
    ]
    in_vmem = pl.BlockSpec(memory_space=pltpu.VMEM)
    return pl.pallas_call(
        functools.partial(layer_kernel, n_seq, n_x),
        out_shape=jax.ShapeDtypeStruct((count, width), BF16),
        in_specs=[in_vmem] * 5 + [pl.BlockSpec(memory_space=pl.ANY)] * 5,
        out_specs=in_vmem,
        scratch_shapes=scratch,
        compiler_params=pltpu.CompilerParams(
            collective_id=0, has_side_effects=True, vmem_limit_bytes=63 * 1024 * 1024
        ),
    )(
        expert_index.T,
        gate_weight.T,
        attn_gain,
        mlp_gain,
        key_value_cache.reshape(length, 128),
        stream_in.T,
        w_qkv.reshape(width, columns),
        w_out.T,
        w_gateup.transpose(0, 2, 3, 1),
        w_down,
    )


def solution(mesh):
    in_specs = (
        P("seq", None),
        P(),
        P(None, "tp", None),
        P(None, "tp", None),
        P("tp", None),
        P(),
        P(("seq", "tp"), None),
        P(("seq", "tp"), None),
        P("seq", None, None, "tp"),
        P("seq", "tp", None),
    )
    out_specs = P(("seq", "tp"), None)
    return jax.shard_map(local, mesh=mesh, in_specs=in_specs, out_specs=out_specs, check_vma=False)
```

```python
import functools

import jax
import jax.numpy as jnp
from jax import lax
from jax.experimental import pallas as pl
from jax.experimental.pallas import tpu as pltpu
from jax.sharding import PartitionSpec as P

HEAD_SIZE = 64
WINDOW_KEYS = 128
TOPK = 4
EPS = 1e-05
MESH = pl.DeviceIdType.MESH
BF16, F32 = jnp.bfloat16, jnp.float32


def rms_scale(values, gain_vec):
    mean_sq = jnp.mean(values * values, axis=-1, keepdims=True)
    return values * lax.rsqrt(mean_sq + EPS) * gain_vec


def contract_last(a, b):
    return lax.dot_general(a, b, (((1,), (1,)), ((), ())), preferred_element_type=F32)


def contract_first(a, b):
    return lax.dot_general(a, b, (((0,), (0,)), ((), ())), preferred_element_type=F32)


class Copies:
    def __init__(self, send_sems):
        self.send_sems = send_sems
        self.started = []

    def start(self, src, dst, recv_sem, seq, tp):
        copy = pltpu.make_async_remote_copy(
            src_ref=src,
            dst_ref=dst,
            send_sem=self.send_sems.at[len(self.started)],
            recv_sem=recv_sem,
            device_id=(seq, tp),
            device_id_type=MESH,
        )
        copy.start()
        self.started.append(copy)

    def drain(self):
        for copy in self.started:
            copy.wait_send()


def arrived(ref, sem):
    pltpu.make_async_copy(ref, ref, sem).wait()


def key_value_sides(keyval):
    keyval = keyval.astype(F32)
    swapped = pltpu.roll(keyval, 64, 1)
    low = lax.broadcasted_iota(jnp.int32, keyval.shape, 1) < HEAD_SIZE
    keys = [jnp.where(low, keyval, 0.0).astype(BF16), jnp.where(low, 0.0, swapped).astype(BF16)]
    values = [jnp.where(low, swapped, 0.0).astype(BF16), jnp.where(low, 0.0, keyval).astype(BF16)]
    return keys, values


def own_scores(projected):
    length = projected.shape[0]
    pairs = projected.shape[1] // 128 - 1
    keys, values = key_value_sides(projected[:, pairs * 128 :])
    queries = jnp.concatenate(
        [projected[:, pair * 128 : (pair + 1) * 128] for pair in range(pairs)], axis=0
    )
    shape = (queries.shape[0], length)
    row = lax.broadcasted_iota(jnp.int32, shape, 0) % length
    later = lax.broadcasted_iota(jnp.int32, shape, 1) > row
    scores = [
        jnp.where(later, -1e30, contract_last(queries, key) * HEAD_SIZE ** (-0.5)) for key in keys
    ]
    return queries, later, scores, values


def window_attention(prepared, earlier):
    queries, later, own, own_values = prepared
    keys, values = key_value_sides(earlier)
    attended = None
    for side in range(2):
        before = contract_last(queries, keys[side]) * HEAD_SIZE ** (-0.5)
        scores = jnp.concatenate([jnp.where(later, before, -1e30), own[side]], axis=1)
        exponent = jnp.exp(scores - jnp.max(scores, axis=-1, keepdims=True))
        weights = (exponent / jnp.sum(exponent, axis=-1, keepdims=True)).astype(BF16)
        both = jnp.concatenate([values[side], own_values[side]], axis=0)
        term = jnp.dot(weights, both, preferred_element_type=F32)
        attended = term if attended is None else attended + term
    attended = attended.astype(BF16)
    length = earlier.shape[0]
    return jnp.concatenate(
        [attended[at : at + length] for at in range(0, attended.shape[0], length)], axis=1
    )


def slot_table(route, core, n_seq, slot_core):
    count = route.shape[1]
    shape = (n_seq * 8, count)
    line = lax.broadcasted_iota(jnp.int32, shape, 0)
    expert = (line // 8 * 2 + core).astype(F32)
    chosen = jnp.zeros(shape, F32)
    weight = jnp.zeros(shape, F32)
    for k in range(TOPK):
        named = expert == route[k : k + 1, :]
        chosen = chosen + named.astype(F32)
        weight = weight + jnp.where(named, route[TOPK + k : TOPK + k + 1, :], 0.0)
    before = lax.broadcasted_iota(jnp.int32, (count, count), 0) < lax.broadcasted_iota(
        jnp.int32, (count, count), 1
    )
    rank = jnp.dot(chosen.astype(BF16), before.astype(BF16), preferred_element_type=F32)
    place = (line % 4).astype(F32)
    here = line % 8 // 4 == slot_core
    hit = jnp.where(here & (rank == place), chosen, 0.0)
    return hit.astype(BF16), hit * weight


def split3(values):
    high = values.astype(BF16)
    rest = values - high.astype(F32)
    middle = rest.astype(BF16)
    return high, middle, (rest - middle.astype(F32)).astype(BF16)


def layer_kernel(
    n_seq,
    n_x,
    index_own,
    weight_own,
    attn_gain,
    mlp_gain,
    cache,
    stream_hbm,
    w_qkv_hbm,
    w_out_hbm,
    w_gateup_hbm,
    w_down_hbm,
    out,
    stream_t,
    w_qkv,
    w_out,
    tail,
    earlier,
    stream,
    route,
    part,
    attn_pair,
    attn_sum,
    attn_opp,
    attn_in,
    residual,
    hidden_a,
    hidden_b,
    packed_a,
    packed_b,
    rows,
    rows_b,
    w_gateup,
    w_down,
    sums,
    product,
    product_b,
    from_pair,
    from_pair_b,
    chip_sum,
    chip_b,
    ring_opp,
    ring_in,
    final,
    returned,
    back_b,
    mixed_b,
    mixed_pair,
    mixed_sum,
    mixed_in_b,
    mixed,
    mixed_in,
    load_sems,
    send_sems,
    attn_sems,
    route_sems,
    hidden_sems,
    block_sems,
    ring_sems,
    pair_sems,
    back_sems,
    opp_sems,
    in_sems,
    home_sems,
    mix_sems,
):
    seq, tp = lax.axis_index("seq"), lax.axis_index("tp")
    x, core = tp // 2, tp % 2
    nz = 4 if n_seq % 4 == 0 else n_seq
    ny = n_seq // nz
    y, z = seq // nz, seq % nz
    partner = tp + 1 - 2 * core
    right_x, left_x, far_x = (x + 1) % n_x, (x + n_x - 1) % n_x, (x + 2) % n_x
    right, left, far = right_x * 2 + core, left_x * 2 + core, far_x * 2 + core
    chunk = max(1, n_seq // 4)
    chunks = n_seq // chunk
    half = chunks // 2
    y_steps = [0, 2, 1, 3] if ny == 4 else list(range(ny))
    first_order = [0, 2, 3, 1] if chunks == 4 else list(range(chunks))
    low_order = list(range(half))[::-1]
    high_order = list(range(half, chunks))
    width = out.shape[-1]
    split = rows.shape[-1]
    length = stream.shape[0] * stream.shape[1]
    copies = Copies(send_sems)

    def load(src, dst, index):
        copy = pltpu.make_async_copy(src, dst, load_sems.at[index])
        copy.start()
        return copy

    edges = [0, width // 3 // 128 * 128, width * 2 // 3 // 128 * 128, width]
    spans = [pl.ds(a, b - a) for a, b in zip(edges[:-1], edges[1:]) if b > a]
    stream_load = load(stream_hbm, stream_t, 0)
    qkv_loads = [
        load(w_qkv_hbm.at[span], w_qkv.at[span], 1 + i) for i, span in enumerate(spans)
    ]
    out_load = load(w_out_hbm, w_out, 4)

    def behind(slot):
        dy, dz = y_steps[slot // nz], slot % nz
        return ((y + ny - dy) % ny) * nz + (z + nz - dz) % nz

    def ahead(slot):
        dy, dz = y_steps[slot // nz], slot % nz
        return ((y + dy) % ny) * nz + (z + dz) % nz

    order = (x, left_x, right_x, far_x)

    def peer(place, other):
        return order[place] * 2 + (1 - core if other else core)

    peers = [peer(place, other) for place in range(4) for other in (True, False)]
    peers = peers[:1] + peers[2:]

    barrier = pltpu.get_barrier_semaphore()
    after = (seq + 1) % n_seq
    for slot in range(1, n_seq):
        pl.semaphore_signal(barrier, inc=1, device_id=(ahead(slot), tp), device_id_type=MESH)
    for other in peers:
        pl.semaphore_signal(barrier, inc=1, device_id=(seq, other), device_id_type=MESH)
    route[tp, 0:TOPK] = index_own[...].astype(F32)
    route[tp, TOPK:] = weight_own[...]

    square = lax.broadcasted_iota(jnp.int32, (length, length), 0)
    eye = (square == lax.broadcasted_iota(jnp.int32, (length, length), 1)).astype(BF16)
    stream_load.wait()
    tokens = contract_last(eye, stream_t[...])
    stream[...] = tokens.astype(BF16).reshape(stream.shape)
    normed = rms_scale(tokens, attn_gain[...].reshape(1, -1)).astype(BF16)
    projected = None
    for span, (a, b), copy in zip(spans, zip(edges[:-1], edges[1:]), qkv_loads):
        copy.wait()
        term = jnp.dot(normed[:, a:b], w_qkv[span], preferred_element_type=F32)
        projected = term if projected is None else projected + term
    projected = projected.astype(BF16)
    tail[...] = projected[:, projected.shape[1] - 128 :]
    pl.semaphore_wait(barrier, n_seq - 1 + len(peers))
    copies.start(tail, earlier, attn_sems.at[0], after, tp)
    for other in peers:
        copies.start(route.at[tp], route.at[tp], route_sems.at[tp], seq, other)
    prepared = own_scores(projected)
    arrived(earlier, attn_sems.at[0])
    attended = window_attention(prepared, jnp.where(seq == 0, cache[...], earlier[...]))
    out_load.wait()
    weight_loads = [load(w_gateup_hbm, w_gateup, 5), load(w_down_hbm, w_down, 6)]
    part[...] = contract_last(attended, w_out[...]).reshape(part.shape).astype(BF16)

    copies.start(part.at[:, 1 - core], attn_pair, attn_sems.at[2], seq, partner)
    for other in peers:
        arrived(route.at[other], route_sems.at[other])
    tables = [
        [slot_table(route[order[place] * 2 + c], core, n_seq, c) for c in range(2)]
        for place in range(4)
    ]
    arrived(attn_pair, attn_sems.at[2])

    def pair_total(peer_x):
        return part[peer_x, core].astype(F32) + attn_pair[peer_x].astype(F32)

    attn_sum[far_x] = pair_total(far_x).astype(BF16)
    copies.start(attn_sum.at[far_x, 0], attn_opp.at[0], attn_sems.at[3], seq, right)
    copies.start(attn_sum.at[far_x, 1], attn_opp.at[1], attn_sems.at[4], seq, left)
    attn_sum[right_x] = pair_total(right_x).astype(BF16)
    copies.start(attn_sum.at[right_x, 1], attn_in.at[0, 1], attn_sems.at[5], seq, right)
    attn_sum[left_x] = pair_total(left_x).astype(BF16)
    copies.start(attn_sum.at[left_x, 0], attn_in.at[1, 0], attn_sems.at[6], seq, left)
    total = stream[tp].astype(F32).reshape(2, -1, width) + pair_total(x)
    arrived(attn_opp.at[0], attn_sems.at[3])
    attn_sum[right_x, 0] = (
        attn_sum[right_x, 0].astype(F32) + attn_opp[0].astype(F32)
    ).astype(BF16)
    copies.start(attn_sum.at[right_x, 0], attn_in.at[0, 0], attn_sems.at[7], seq, right)
    arrived(attn_opp.at[1], attn_sems.at[4])
    attn_sum[left_x, 1] = (
        attn_sum[left_x, 1].astype(F32) + attn_opp[1].astype(F32)
    ).astype(BF16)
    copies.start(attn_sum.at[left_x, 1], attn_in.at[1, 1], attn_sems.at[8], seq, left)
    for which, part_of, sem in ((0, 1, 5), (1, 0, 6), (0, 0, 7), (1, 1, 8)):
        arrived(attn_in.at[which, part_of], attn_sems.at[sem])
    total = (total + attn_in[0].astype(F32) + attn_in[1].astype(F32)).reshape(-1, width)
    residual[...] = total
    normed = rms_scale(total, mlp_gain[...].reshape(1, -1)).astype(BF16)
    hidden_a[core] = normed[:, :split]
    hidden_b[tp] = normed[:, split:]
    copies.start(hidden_a.at[core], hidden_a.at[core], attn_sems.at[9], seq, partner)
    for other in peers:
        copies.start(hidden_b.at[tp], hidden_b.at[tp], hidden_sems.at[tp], seq, other)
    arrived(hidden_a.at[1 - core], attn_sems.at[9])

    def pack(place, first, second):
        both = jnp.dot(tables[place][0][0], first, preferred_element_type=F32) + jnp.dot(
            tables[place][1][0], second, preferred_element_type=F32
        )
        return both.reshape(n_seq, 8, -1).astype(BF16)

    packed_a[...] = pack(0, hidden_a[0], hidden_a[1])
    for group in first_order:
        for slot in range(group * chunk, (group + 1) * chunk):
            if slot:
                holder = behind(slot)
                copies.start(
                    packed_a.at[holder], rows.at[core, x, slot], block_sems.at[0, group], holder, tp
                )
    rows[core, x, 0] = packed_a[seq]
    for other in peers:
        arrived(hidden_b.at[other], hidden_sems.at[other])
    for place in range(4):
        packed_b[:, place] = pack(
            place, hidden_b[order[place] * 2], hidden_b[order[place] * 2 + 1]
        )
    for group in first_order:
        for slot in range(group * chunk, (group + 1) * chunk):
            if slot:
                holder = behind(slot)
                copies.start(
                    packed_b.at[holder], rows_b.at[core, slot], block_sems.at[1, group], holder, tp
                )
    rows_b[core, 0] = packed_b[seq]

    def slots(group):
        return pl.ds(group * chunk, chunk)

    def spread(group):
        first = 1 if group == 0 else 0
        if chunk > first:
            got = rows.at[core, x, pl.ds(group * chunk + first, chunk - first)]
            arrived(got, block_sems.at[0, group])
        own = rows.at[core, x, slots(group)]
        copies.start(own, own, ring_sems.at[0, group], seq, right)
        copies.start(own, own, ring_sems.at[1, group], seq, left)
        copies.start(own, own, pair_sems.at[0, group], seq, partner)

    done = set()

    def take(from_left, group):
        if (from_left, group) in done:
            return
        done.add((from_left, group))
        got = rows.at[core, left_x if from_left else right_x, slots(group)]
        arrived(got, ring_sems.at[0 if from_left else 1, group])
        if from_left and group < half:
            copies.start(got, got, ring_sems.at[2, group], seq, right)
        if not from_left and group >= half:
            copies.start(got, got, ring_sems.at[2, group], seq, left)
        copies.start(got, got, pair_sems.at[1 if from_left else 2, group], seq, partner)

    def take_b(group):
        first = 1 if group == 0 else 0
        if chunk > first:
            got = rows_b.at[core, pl.ds(group * chunk + first, chunk - first)]
            arrived(got, block_sems.at[1, group])
        own = rows_b.at[core, slots(group)]
        copies.start(own, own, pair_sems.at[4, group], seq, partner)

    def entered(place, expert, which):
        taken = rows[expert, order[place]].reshape(n_seq * 8, split)
        return contract_last(taken, w_gateup[expert, which, :, 0:split])

    def enter(place):
        for group in range(chunks):
            arrived(rows.at[1 - core, order[place], slots(group)], pair_sems.at[place, group])

    def early(place):
        enter(place)

        def one(expert, carry):
            for which in range(2):
                sums[expert, place, which] = entered(place, expert, which)
            return carry

        lax.fori_loop(0, 2, one, 0)

    def finish(place, expert, gate, up):
        taken = rows_b[expert, :, place].reshape(n_seq * 8, width - split)
        gate = gate + contract_last(taken, w_gateup[expert, 0, :, split:])
        up = up + contract_last(taken, w_gateup[expert, 1, :, split:])
        activated = (gate / (1.0 + jnp.exp(-gate)) * up).astype(BF16)
        result = jnp.dot(activated, w_down[expert], preferred_element_type=F32)
        result = result.reshape(n_seq, 8, width).astype(BF16)
        product[expert, order[place]] = result[:, :, :split]
        product_b[expert, :, place] = result[:, :, split:]

    def block(place, ready):
        def one(expert):
            if ready:
                gate, up = sums[expert, place, 0], sums[expert, place, 1]
            else:
                gate, up = entered(place, expert, 0), entered(place, expert, 1)
            finish(place, expert, gate, up)

        one(1 - core)
        block_x = order[place]
        for group in range(chunks):
            copies.start(
                product.at[1 - core, block_x, slots(group)],
                from_pair.at[block_x, slots(group)],
                back_sems.at[place, group],
                seq,
                partner,
            )
        copies.start(
            product_b.at[1 - core, :, place],
            from_pair_b.at[:, place],
            mix_sems.at[place],
            seq,
            partner,
        )
        one(core)

    def pair_sum_b(places):
        for place in places:
            arrived(from_pair_b.at[:, place], mix_sems.at[place])
            chip_b[:, place] = (
                product_b[core, :, place].astype(F32) + from_pair_b[:, place].astype(F32)
            ).astype(BF16)
        span = pl.ds(places[0], len(places))
        which = 0 if places[0] == 0 else 1
        for group in first_order:
            for slot in range(group * chunk, (group + 1) * chunk):
                if slot:
                    copies.start(
                        chip_b.at[slot, span],
                        back_b.at[seq, span],
                        home_sems.at[1 + which, slot],
                        ahead(slot),
                        tp,
                    )
        back_b[seq, span] = chip_b[0, span]

    def pair_sum(block_x, which, group):
        at = slots(group)
        arrived(from_pair.at[block_x, at], back_sems.at[which, group])
        chip_sum[block_x, at] = (
            product[core, block_x, at].astype(F32) + from_pair[block_x, at].astype(F32)
        ).astype(BF16)

    for group in first_order[:-1]:
        spread(group)
    take(True, 0)
    if half in first_order[:-1]:
        take(False, half)
    spread(first_order[-1])
    take(False, chunks - 1)
    for copy in weight_loads:
        copy.wait()
    early(0)
    for group in first_order:
        take(True, group)
        take(False, group)
    for group in first_order:
        take_b(group)
    early(1)
    early(2)
    for group in first_order:
        arrived(rows_b.at[1 - core, slots(group)], pair_sems.at[4, group])
    block(0, True)
    block(1, True)
    block(2, True)
    for group in high_order:
        pair_sum(right_x, 2, group)
        copies.start(
            chip_sum.at[right_x, slots(group)],
            ring_in.at[0, slots(group)],
            in_sems.at[0, group],
            seq,
            right,
        )
    for group in low_order:
        pair_sum(left_x, 1, group)
        copies.start(
            chip_sum.at[left_x, slots(group)],
            ring_in.at[1, slots(group)],
            in_sems.at[1, group],
            seq,
            left,
        )

    for group in range(chunks):
        got = rows.at[core, far_x, slots(group)]
        arrived(got, ring_sems.at[2, group])
        copies.start(got, got, pair_sems.at[3, group], seq, partner)
    pair_sum_b((0, 1, 2))
    enter(3)
    block(3, False)
    for low, high in zip(low_order, high_order):
        pair_sum(far_x, 3, low)
        copies.start(
            chip_sum.at[far_x, slots(low)], ring_opp.at[slots(low)], opp_sems.at[low], seq, right
        )
        pair_sum(far_x, 3, high)
        copies.start(
            chip_sum.at[far_x, slots(high)], ring_opp.at[slots(high)], opp_sems.at[high], seq, left
        )
    for low, high in zip(low_order, high_order):
        pair_sum(right_x, 2, low)
        pair_sum(left_x, 1, high)
        pair_sum(x, 0, low)
        pair_sum(x, 0, high)
    pair_sum_b((3,))
    for low, high in zip(low_order, high_order):
        for group, peer_x, target, side in ((low, right_x, right, 0), (high, left_x, left, 1)):
            at = slots(group)
            arrived(ring_opp.at[at], opp_sems.at[group])
            chip_sum[peer_x, at] = (
                chip_sum[peer_x, at].astype(F32) + ring_opp[at].astype(F32)
            ).astype(BF16)
            copies.start(
                chip_sum.at[peer_x, at], ring_in.at[side, at], in_sems.at[side, group], seq, target
            )

    pickers = [[split3(tables[place][c][1]) for c in range(2)] for place in range(4)]

    def mixture(place, c, terms):
        return sum(contract_first(piece, terms) for piece in pickers[place][c])

    def home(group):
        at = slots(group)
        arrived(ring_in.at[0, at], in_sems.at[0, group])
        arrived(ring_in.at[1, at], in_sems.at[1, group])
        final[at] = (
            chip_sum[x, at].astype(F32) + ring_in[0, at].astype(F32) + ring_in[1, at].astype(F32)
        ).astype(BF16)
        for slot in range(group * chunk, (group + 1) * chunk):
            if slot:
                copies.start(
                    final.at[slot], returned.at[seq], home_sems.at[0, slot], ahead(slot), tp
                )

    def mix_b(places):
        span = pl.ds(places[0], len(places))
        which = 0 if places[0] == 0 else 1
        for slot in range(1, n_seq):
            arrived(back_b.at[behind(slot), span], home_sems.at[1 + which, slot])
        for place in places:
            terms = back_b[:, place].reshape(n_seq * 8, width - split)
            for c in range(2):
                mixed_b[c, place] = mixture(place, c, terms).astype(BF16)

    mix_b((0, 1, 2))
    home(low_order[0])
    home(high_order[0])
    mix_b((3,))
    copies.start(mixed_b.at[1 - core], mixed_pair, attn_sems.at[11], seq, partner)
    arrived(mixed_pair, attn_sems.at[11])
    for place in (3, 1, 2):
        mixed_sum[place - 1] = (
            mixed_b[core, place].astype(F32) + mixed_pair[place].astype(F32)
        ).astype(BF16)
        copies.start(
            mixed_sum.at[place - 1],
            mixed_in_b.at[place - 1],
            attn_sems.at[11 + place],
            seq,
            peer(place, False),
        )
    for low, high in zip(low_order[1:], high_order[1:]):
        home(low)
        home(high)
    returned[seq] = final[0]
    total_b = mixed_b[core, 0].astype(F32) + mixed_pair[0].astype(F32)
    for place in (1, 2, 3):
        arrived(mixed_in_b.at[place - 1], attn_sems.at[11 + place])
        total_b = total_b + mixed_in_b[place - 1].astype(F32)
    residual[:, split:] = residual[:, split:] + total_b
    for slot in range(1, n_seq):
        arrived(returned.at[behind(slot)], home_sems.at[0, slot])
    terms = returned[...].reshape(n_seq * 8, split)
    for c in range(2):
        mixed[c] = mixture(0, c, terms)
    copies.start(mixed.at[1 - core], mixed_in, attn_sems.at[10], seq, partner)
    out[:, split:] = residual[:, split:].astype(BF16)
    arrived(mixed_in, attn_sems.at[10])
    out[:, :split] = (residual[:, :split] + (mixed[core] + mixed_in[...])).astype(BF16)
    copies.drain()


def local(
    stream_in,
    attn_gain,
    w_qkv,
    key_value_cache,
    w_out,
    mlp_gain,
    expert_index,
    gate_weight,
    w_gateup,
    w_down,
):
    n_seq = lax.axis_size("seq")
    n_tp = lax.axis_size("tp")
    n_x = n_tp // 2
    length, width = stream_in.shape
    count = length // n_tp
    hidden = w_down.shape[1]
    columns = w_qkv.shape[2]
    heads_width = w_out.shape[0]
    vmem, dma = pltpu.VMEM, pltpu.SemaphoreType.DMA
    chunks = n_seq // max(1, n_seq // 4)
    split = width * 2 // 3 // 128 * 128
    rest = width - split
    scratch = [
        vmem((width, length), BF16),
        vmem((width, columns), BF16),
        vmem((width, heads_width), BF16),
        vmem((length, 128), BF16),
        vmem((length, 128), BF16),
        vmem((n_tp, count, width), BF16),
        vmem((n_tp, 2 * TOPK, count), F32),
        vmem((n_x, 2, 2, count // 2, width), BF16),
        vmem((n_x, 2, count // 2, width), BF16),
        vmem((n_x, 2, count // 2, width), BF16),
        vmem((2, count // 2, width), BF16),
        vmem((2, 2, count // 2, width), BF16),
        vmem((count, width), F32),
        vmem((2, count, split), BF16),
        vmem((n_tp, count, rest), BF16),
        vmem((n_seq, 8, split), BF16),
        vmem((n_seq, n_x, 8, rest), BF16),
        vmem((2, n_x, n_seq, 8, split), BF16),
        vmem((2, n_seq, n_x, 8, rest), BF16),
        vmem((2, 2, hidden, width), BF16),
        vmem((2, hidden, width), BF16),
        vmem((2, 3, 2, n_seq * 8, hidden), F32),
        vmem((2, n_x, n_seq, 8, split), BF16),
        vmem((2, n_seq, n_x, 8, rest), BF16),
        vmem((n_x, n_seq, 8, split), BF16),
        vmem((n_seq, n_x, 8, rest), BF16),
        vmem((n_x, n_seq, 8, split), BF16),
        vmem((n_seq, n_x, 8, rest), BF16),
        vmem((n_seq, 8, split), BF16),
        vmem((2, n_seq, 8, split), BF16),
        vmem((n_seq, 8, split), BF16),
        vmem((n_seq, 8, split), BF16),
        vmem((n_seq, n_x, 8, rest), BF16),
        vmem((2, n_x, count, rest), BF16),
        vmem((n_x, count, rest), BF16),
        vmem((3, count, rest), BF16),
        vmem((3, count, rest), BF16),
        vmem((2, count, split), F32),
        vmem((count, split), F32),
        dma((7,)),
        dma((256,)),
        dma((15,)),
        dma((n_tp,)),
        dma((n_tp,)),
        dma((2, chunks)),
        dma((3, chunks)),
        dma((5, chunks)),
        dma((4, chunks)),
        dma((chunks,)),
        dma((2, chunks)),
        dma((3, n_seq)),
        dma((4,)),
    ]
    in_vmem = pl.BlockSpec(memory_space=pltpu.VMEM)
    return pl.pallas_call(
        functools.partial(layer_kernel, n_seq, n_x),
        out_shape=jax.ShapeDtypeStruct((count, width), BF16),
        in_specs=[in_vmem] * 5 + [pl.BlockSpec(memory_space=pl.ANY)] * 5,
        out_specs=in_vmem,
        scratch_shapes=scratch,
        compiler_params=pltpu.CompilerParams(
            collective_id=0, has_side_effects=True, vmem_limit_bytes=63 * 1024 * 1024
        ),
    )(
        expert_index.T,
        gate_weight.T,
        attn_gain,
        mlp_gain,
        key_value_cache.reshape(length, 128),
        stream_in.T,
        w_qkv.reshape(width, columns),
        w_out.T,
        w_gateup.transpose(0, 2, 3, 1),
        w_down,
    )


def solution(mesh):
    in_specs = (
        P("seq", None),
        P(),
        P(None, "tp", None),
        P(None, "tp", None),
        P("tp", None),
        P(),
        P(("seq", "tp"), None),
        P(("seq", "tp"), None),
        P("seq", None, None, "tp"),
        P("seq", "tp", None),
    )
    out_specs = P(("seq", "tp"), None)
    return jax.shard_map(local, mesh=mesh, in_specs=in_specs, out_specs=out_specs, check_vma=False)
```

```python
import functools

import jax
import jax.numpy as jnp
from jax import lax
from jax.experimental import pallas as pl
from jax.experimental.pallas import tpu as pltpu
from jax.sharding import PartitionSpec as P

HEAD_SIZE = 64
WINDOW_KEYS = 128
TOPK = 4
EPS = 1e-05
MESH = pl.DeviceIdType.MESH
BF16, F32 = jnp.bfloat16, jnp.float32


def rms_scale(values, gain_vec):
    mean_sq = jnp.mean(values * values, axis=-1, keepdims=True)
    return values * lax.rsqrt(mean_sq + EPS) * gain_vec


def contract_last(a, b):
    return lax.dot_general(a, b, (((1,), (1,)), ((), ())), preferred_element_type=F32)


def contract_first(a, b):
    return lax.dot_general(a, b, (((0,), (0,)), ((), ())), preferred_element_type=F32)


class Copies:
    def __init__(self, send_sems):
        self.send_sems = send_sems
        self.started = []

    def start(self, src, dst, recv_sem, seq, tp):
        copy = pltpu.make_async_remote_copy(
            src_ref=src,
            dst_ref=dst,
            send_sem=self.send_sems.at[len(self.started)],
            recv_sem=recv_sem,
            device_id=(seq, tp),
            device_id_type=MESH,
        )
        copy.start()
        self.started.append(copy)

    def drain(self):
        for copy in self.started:
            copy.wait_send()


def arrived(ref, sem):
    pltpu.make_async_copy(ref, ref, sem).wait()


def key_value_sides(keyval):
    keyval = keyval.astype(F32)
    swapped = pltpu.roll(keyval, 64, 1)
    low = lax.broadcasted_iota(jnp.int32, keyval.shape, 1) < HEAD_SIZE
    keys = [jnp.where(low, keyval, 0.0).astype(BF16), jnp.where(low, 0.0, swapped).astype(BF16)]
    values = [jnp.where(low, swapped, 0.0).astype(BF16), jnp.where(low, 0.0, keyval).astype(BF16)]
    return keys, values


def own_scores(projected):
    length = projected.shape[0]
    pairs = projected.shape[1] // 128 - 1
    keys, values = key_value_sides(projected[:, pairs * 128 :])
    queries = jnp.concatenate(
        [projected[:, pair * 128 : (pair + 1) * 128] for pair in range(pairs)], axis=0
    )
    shape = (queries.shape[0], length)
    row = lax.broadcasted_iota(jnp.int32, shape, 0) % length
    later = lax.broadcasted_iota(jnp.int32, shape, 1) > row
    scores = [
        jnp.where(later, -1e30, contract_last(queries, key) * HEAD_SIZE ** (-0.5)) for key in keys
    ]
    return queries, later, scores, values


def window_attention(prepared, earlier):
    queries, later, own, own_values = prepared
    keys, values = key_value_sides(earlier)
    attended = None
    for side in range(2):
        before = contract_last(queries, keys[side]) * HEAD_SIZE ** (-0.5)
        scores = jnp.concatenate([jnp.where(later, before, -1e30), own[side]], axis=1)
        exponent = jnp.exp(scores - jnp.max(scores, axis=-1, keepdims=True))
        weights = (exponent / jnp.sum(exponent, axis=-1, keepdims=True)).astype(BF16)
        both = jnp.concatenate([values[side], own_values[side]], axis=0)
        term = jnp.dot(weights, both, preferred_element_type=F32)
        attended = term if attended is None else attended + term
    attended = attended.astype(BF16)
    length = earlier.shape[0]
    return jnp.concatenate(
        [attended[at : at + length] for at in range(0, attended.shape[0], length)], axis=1
    )


def slot_tables(routes, core, n_seq):
    count = routes[0].shape[1]
    route = jnp.concatenate(routes, axis=1)
    shape = (n_seq * 8, route.shape[1])
    line = lax.broadcasted_iota(jnp.int32, shape, 0)
    token = lax.broadcasted_iota(jnp.int32, shape, 1)
    expert = (line // 8 * 2 + core).astype(F32)
    chosen = jnp.zeros(shape, F32)
    weight = jnp.zeros(shape, F32)
    for k in range(TOPK):
        named = expert == route[k : k + 1, :]
        chosen = chosen + named.astype(F32)
        weight = weight + jnp.where(named, route[TOPK + k : TOPK + k + 1, :], 0.0)
    square = (shape[1], shape[1])
    one = lax.broadcasted_iota(jnp.int32, square, 0)
    two = lax.broadcasted_iota(jnp.int32, square, 1)
    before = (one < two) & (one // count == two // count)
    rank = jnp.dot(
        chosen.astype(BF16), before.astype(F32).astype(BF16), preferred_element_type=F32
    )
    place = (line % 4).astype(F32)
    here = line % 8 // 4 == token // count % 2
    hit = jnp.where(here & (rank == place), chosen, 0.0)
    return hit.astype(BF16), hit * weight


def split3(values):
    high = values.astype(BF16)
    rest = values - high.astype(F32)
    middle = rest.astype(BF16)
    return high, middle, (rest - middle.astype(F32)).astype(BF16)


def layer_kernel(
    n_seq,
    n_x,
    index_own,
    weight_own,
    attn_gain,
    mlp_gain,
    cache,
    stream_hbm,
    w_qkv_hbm,
    w_out_hbm,
    w_gateup_hbm,
    w_down_hbm,
    out,
    stream_t,
    w_qkv,
    w_out,
    tail,
    earlier,
    stream,
    route,
    part,
    attn_pair,
    attn_sum,
    attn_opp,
    attn_in,
    residual,
    hidden_a,
    hidden_b,
    pickers,
    packed_a,
    packed_b,
    rows,
    rows_b,
    w_gateup,
    w_down,
    sums,
    product,
    product_b,
    from_pair,
    from_pair_b,
    chip_sum,
    chip_b,
    ring_opp,
    ring_in,
    final,
    returned,
    back_b,
    mixed_b,
    mixed_pair,
    mixed_sum,
    mixed_in_b,
    mixed,
    mixed_in,
    load_sems,
    send_sems,
    attn_sems,
    route_sems,
    hidden_sems,
    block_sems,
    ring_sems,
    pair_sems,
    back_sems,
    opp_sems,
    in_sems,
    home_sems,
    mix_sems,
):
    seq, tp = lax.axis_index("seq"), lax.axis_index("tp")
    x, core = tp // 2, tp % 2
    nz = 4 if n_seq % 4 == 0 else n_seq
    ny = n_seq // nz
    y, z = seq // nz, seq % nz
    partner = tp + 1 - 2 * core
    right_x, left_x, far_x = (x + 1) % n_x, (x + n_x - 1) % n_x, (x + 2) % n_x
    right, left, far = right_x * 2 + core, left_x * 2 + core, far_x * 2 + core
    chunk = max(1, n_seq // 4)
    chunks = n_seq // chunk
    half = chunks // 2
    y_steps = [0, 2, 1, 3] if ny == 4 else list(range(ny))
    first_order = [0, 2, 3, 1] if chunks == 4 else list(range(chunks))
    low_order = list(range(half))[::-1]
    high_order = list(range(half, chunks))
    width = out.shape[-1]
    split = rows.shape[-1]
    length = stream.shape[0] * stream.shape[1]
    copies = Copies(send_sems)

    def load(src, dst, index):
        copy = pltpu.make_async_copy(src, dst, load_sems.at[index])
        copy.start()
        return copy

    edges = [0, width // 3 // 128 * 128, width * 2 // 3 // 128 * 128, width]
    spans = [pl.ds(a, b - a) for a, b in zip(edges[:-1], edges[1:]) if b > a]
    stream_load = load(stream_hbm, stream_t, 0)
    qkv_loads = [
        load(w_qkv_hbm.at[span], w_qkv.at[span], 1 + i) for i, span in enumerate(spans)
    ]
    out_load = load(w_out_hbm, w_out, 4)

    def behind(slot):
        dy, dz = y_steps[slot // nz], slot % nz
        return ((y + ny - dy) % ny) * nz + (z + nz - dz) % nz

    def ahead(slot):
        dy, dz = y_steps[slot // nz], slot % nz
        return ((y + dy) % ny) * nz + (z + dz) % nz

    order = (x, left_x, right_x, far_x)

    def peer(place, other):
        return order[place] * 2 + (1 - core if other else core)

    peers = [peer(place, other) for place in range(4) for other in (True, False)]
    peers = peers[:1] + peers[2:]

    barrier = pltpu.get_barrier_semaphore()
    after = (seq + 1) % n_seq
    for slot in range(1, n_seq):
        pl.semaphore_signal(barrier, inc=1, device_id=(ahead(slot), tp), device_id_type=MESH)
    for other in peers:
        pl.semaphore_signal(barrier, inc=1, device_id=(seq, other), device_id_type=MESH)
    route[tp, 0:TOPK] = index_own[...].astype(F32)
    route[tp, TOPK:] = weight_own[...]

    square = lax.broadcasted_iota(jnp.int32, (length, length), 0)
    eye = (square == lax.broadcasted_iota(jnp.int32, (length, length), 1)).astype(BF16)
    stream_load.wait()
    tokens = contract_last(eye, stream_t[...])
    stream[...] = tokens.astype(BF16).reshape(stream.shape)
    normed = rms_scale(tokens, attn_gain[...].reshape(1, -1)).astype(BF16)
    projected = None
    for span, (a, b), copy in zip(spans, zip(edges[:-1], edges[1:]), qkv_loads):
        copy.wait()
        term = jnp.dot(normed[:, a:b], w_qkv[span], preferred_element_type=F32)
        projected = term if projected is None else projected + term
    projected = projected.astype(BF16)
    tail[...] = projected[:, projected.shape[1] - 128 :]
    pl.semaphore_wait(barrier, n_seq - 1 + len(peers))
    copies.start(tail, earlier, attn_sems.at[0], after, tp)
    for other in peers:
        copies.start(route.at[tp], route.at[tp], route_sems.at[tp], seq, other)
    prepared = own_scores(projected)
    arrived(earlier, attn_sems.at[0])
    attended = window_attention(prepared, jnp.where(seq == 0, cache[...], earlier[...]))
    out_load.wait()
    weight_loads = [load(w_gateup_hbm, w_gateup, 5), load(w_down_hbm, w_down, 6)]
    part[...] = contract_last(attended, w_out[...]).reshape(part.shape).astype(BF16)

    copies.start(part.at[:, 1 - core], attn_pair, attn_sems.at[2], seq, partner)
    for other in peers:
        arrived(route.at[other], route_sems.at[other])
    placer, weighted = slot_tables(
        [route[order[place] * 2 + c] for place in range(4) for c in range(2)], core, n_seq
    )
    wide = 2 * out.shape[0]
    placers = [placer[:, place * wide : (place + 1) * wide] for place in range(4)]
    pieces = split3(weighted)
    for place in range(4):
        pickers[place] = jnp.concatenate(
            [piece[:, place * wide : (place + 1) * wide] for piece in pieces], axis=1
        )
    arrived(attn_pair, attn_sems.at[2])

    def pair_total(peer_x):
        return part[peer_x, core].astype(F32) + attn_pair[peer_x].astype(F32)

    attn_sum[far_x] = pair_total(far_x).astype(BF16)
    copies.start(attn_sum.at[far_x, 0], attn_opp.at[0], attn_sems.at[3], seq, right)
    copies.start(attn_sum.at[far_x, 1], attn_opp.at[1], attn_sems.at[4], seq, left)
    attn_sum[right_x] = pair_total(right_x).astype(BF16)
    copies.start(attn_sum.at[right_x, 1], attn_in.at[0, 1], attn_sems.at[5], seq, right)
    attn_sum[left_x] = pair_total(left_x).astype(BF16)
    copies.start(attn_sum.at[left_x, 0], attn_in.at[1, 0], attn_sems.at[6], seq, left)
    total = stream[tp].astype(F32).reshape(2, -1, width) + pair_total(x)
    arrived(attn_opp.at[0], attn_sems.at[3])
    attn_sum[right_x, 0] = (
        attn_sum[right_x, 0].astype(F32) + attn_opp[0].astype(F32)
    ).astype(BF16)
    copies.start(attn_sum.at[right_x, 0], attn_in.at[0, 0], attn_sems.at[7], seq, right)
    arrived(attn_opp.at[1], attn_sems.at[4])
    attn_sum[left_x, 1] = (
        attn_sum[left_x, 1].astype(F32) + attn_opp[1].astype(F32)
    ).astype(BF16)
    copies.start(attn_sum.at[left_x, 1], attn_in.at[1, 1], attn_sems.at[8], seq, left)
    for which, part_of, sem in ((0, 1, 5), (1, 0, 6), (0, 0, 7), (1, 1, 8)):
        arrived(attn_in.at[which, part_of], attn_sems.at[sem])
    total = (total + attn_in[0].astype(F32) + attn_in[1].astype(F32)).reshape(-1, width)
    residual[...] = total
    normed = rms_scale(total, mlp_gain[...].reshape(1, -1)).astype(BF16)
    hidden_a[core] = normed[:, :split]
    hidden_b[tp] = normed[:, split:]
    copies.start(hidden_a.at[core], hidden_a.at[core], attn_sems.at[9], seq, partner)
    for other in peers:
        copies.start(hidden_b.at[tp], hidden_b.at[tp], hidden_sems.at[tp], seq, other)
    arrived(hidden_a.at[1 - core], attn_sems.at[9])

    def pack(place, both):
        taken = jnp.dot(
            placers[place], both.reshape(wide, -1), preferred_element_type=F32
        )
        return taken.reshape(n_seq, 8, -1).astype(BF16)

    packed_a[...] = pack(0, hidden_a[...])
    for group in first_order:
        for slot in range(group * chunk, (group + 1) * chunk):
            if slot:
                holder = behind(slot)
                copies.start(
                    packed_a.at[holder], rows.at[core, x, slot], block_sems.at[0, group], holder, tp
                )
    rows[core, x, 0] = packed_a[seq]
    for other in peers:
        arrived(hidden_b.at[other], hidden_sems.at[other])
    for place in range(4):
        packed_b[:, place] = pack(place, hidden_b[pl.ds(order[place] * 2, 2)])
    for group in first_order:
        for slot in range(group * chunk, (group + 1) * chunk):
            if slot:
                holder = behind(slot)
                copies.start(
                    packed_b.at[holder], rows_b.at[core, slot], block_sems.at[1, group], holder, tp
                )
    rows_b[core, 0] = packed_b[seq]

    def slots(group):
        return pl.ds(group * chunk, chunk)

    def spread(group):
        first = 1 if group == 0 else 0
        if chunk > first:
            got = rows.at[core, x, pl.ds(group * chunk + first, chunk - first)]
            arrived(got, block_sems.at[0, group])
        own = rows.at[core, x, slots(group)]
        copies.start(own, own, ring_sems.at[0, group], seq, right)
        copies.start(own, own, ring_sems.at[1, group], seq, left)
        copies.start(own, own, pair_sems.at[0, group], seq, partner)

    done = set()

    def take(from_left, group):
        if (from_left, group) in done:
            return
        done.add((from_left, group))
        got = rows.at[core, left_x if from_left else right_x, slots(group)]
        arrived(got, ring_sems.at[0 if from_left else 1, group])
        if from_left and group < half:
            copies.start(got, got, ring_sems.at[2, group], seq, right)
        if not from_left and group >= half:
            copies.start(got, got, ring_sems.at[2, group], seq, left)
        copies.start(got, got, pair_sems.at[1 if from_left else 2, group], seq, partner)

    def take_b(group):
        first = 1 if group == 0 else 0
        if chunk > first:
            got = rows_b.at[core, pl.ds(group * chunk + first, chunk - first)]
            arrived(got, block_sems.at[1, group])
        own = rows_b.at[core, slots(group)]
        copies.start(own, own, pair_sems.at[4, group], seq, partner)

    def entered(place, expert, which):
        taken = rows[expert, order[place]].reshape(n_seq * 8, split)
        return contract_last(taken, w_gateup[expert, which, :, 0:split])

    def enter(place):
        for group in range(chunks):
            arrived(rows.at[1 - core, order[place], slots(group)], pair_sems.at[place, group])

    def early(place):
        enter(place)

        def one(expert, carry):
            for which in range(2):
                sums[expert, place, which] = entered(place, expert, which)
            return carry

        lax.fori_loop(0, 2, one, 0)

    def finish(place, expert, gate, up):
        taken = rows_b[expert, :, place].reshape(n_seq * 8, width - split)
        gate = gate + contract_last(taken, w_gateup[expert, 0, :, split:])
        up = up + contract_last(taken, w_gateup[expert, 1, :, split:])
        activated = (gate / (1.0 + jnp.exp(-gate)) * up).astype(BF16)
        result = jnp.dot(activated, w_down[expert], preferred_element_type=F32)
        result = result.reshape(n_seq, 8, width).astype(BF16)
        product[expert, order[place]] = result[:, :, :split]
        product_b[expert, :, place] = result[:, :, split:]

    def block(place, ready):
        def one(expert):
            if ready:
                gate, up = sums[expert, place, 0], sums[expert, place, 1]
            else:
                gate, up = entered(place, expert, 0), entered(place, expert, 1)
            finish(place, expert, gate, up)

        one(1 - core)
        block_x = order[place]
        for group in range(chunks):
            copies.start(
                product.at[1 - core, block_x, slots(group)],
                from_pair.at[block_x, slots(group)],
                back_sems.at[place, group],
                seq,
                partner,
            )
        copies.start(
            product_b.at[1 - core, :, place],
            from_pair_b.at[:, place],
            mix_sems.at[place],
            seq,
            partner,
        )
        one(core)

    def pair_sum_b(places):
        for place in places:
            arrived(from_pair_b.at[:, place], mix_sems.at[place])
            chip_b[:, place] = (
                product_b[core, :, place].astype(F32) + from_pair_b[:, place].astype(F32)
            ).astype(BF16)
        span = pl.ds(places[0], len(places))
        which = 0 if places[0] == 0 else 1
        for group in first_order:
            for slot in range(group * chunk, (group + 1) * chunk):
                if slot:
                    copies.start(
                        chip_b.at[slot, span],
                        back_b.at[seq, span],
                        home_sems.at[1 + which, slot],
                        ahead(slot),
                        tp,
                    )
        back_b[seq, span] = chip_b[0, span]

    def pair_sum(block_x, which, group):
        at = slots(group)
        arrived(from_pair.at[block_x, at], back_sems.at[which, group])
        chip_sum[block_x, at] = (
            product[core, block_x, at].astype(F32) + from_pair[block_x, at].astype(F32)
        ).astype(BF16)

    for group in first_order[:-1]:
        spread(group)
    take(True, 0)
    if half in first_order[:-1]:
        take(False, half)
    spread(first_order[-1])
    take(False, chunks - 1)
    for copy in weight_loads:
        copy.wait()
    early(0)
    for group in first_order:
        take(True, group)
        take(False, group)
    for group in first_order:
        take_b(group)
    early(1)
    early(2)
    for group in first_order:
        arrived(rows_b.at[1 - core, slots(group)], pair_sems.at[4, group])
    block(0, True)
    block(1, True)
    block(2, True)
    for group in high_order:
        pair_sum(right_x, 2, group)
        copies.start(
            chip_sum.at[right_x, slots(group)],
            ring_in.at[0, slots(group)],
            in_sems.at[0, group],
            seq,
            right,
        )
    for group in low_order:
        pair_sum(left_x, 1, group)
        copies.start(
            chip_sum.at[left_x, slots(group)],
            ring_in.at[1, slots(group)],
            in_sems.at[1, group],
            seq,
            left,
        )

    for group in range(chunks):
        got = rows.at[core, far_x, slots(group)]
        arrived(got, ring_sems.at[2, group])
        copies.start(got, got, pair_sems.at[3, group], seq, partner)
    pair_sum_b((0, 1, 2))
    enter(3)
    block(3, False)
    for low, high in zip(low_order, high_order):
        pair_sum(far_x, 3, low)
        copies.start(
            chip_sum.at[far_x, slots(low)], ring_opp.at[slots(low)], opp_sems.at[low], seq, right
        )
        pair_sum(far_x, 3, high)
        copies.start(
            chip_sum.at[far_x, slots(high)], ring_opp.at[slots(high)], opp_sems.at[high], seq, left
        )
    for low, high in zip(low_order, high_order):
        pair_sum(right_x, 2, low)
        pair_sum(left_x, 1, high)
        pair_sum(x, 0, low)
        pair_sum(x, 0, high)
    pair_sum_b((3,))
    for low, high in zip(low_order, high_order):
        for group, peer_x, target, side in ((low, right_x, right, 0), (high, left_x, left, 1)):
            at = slots(group)
            arrived(ring_opp.at[at], opp_sems.at[group])
            chip_sum[peer_x, at] = (
                chip_sum[peer_x, at].astype(F32) + ring_opp[at].astype(F32)
            ).astype(BF16)
            copies.start(
                chip_sum.at[peer_x, at], ring_in.at[side, at], in_sems.at[side, group], seq, target
            )

    def mixture(place, terms):
        parts = contract_first(pickers[place], terms)
        whole = parts[:wide] + parts[wide : 2 * wide] + parts[2 * wide :]
        return whole.reshape(2, wide // 2, -1)

    def home(group):
        at = slots(group)
        arrived(ring_in.at[0, at], in_sems.at[0, group])
        arrived(ring_in.at[1, at], in_sems.at[1, group])
        final[at] = (
            chip_sum[x, at].astype(F32) + ring_in[0, at].astype(F32) + ring_in[1, at].astype(F32)
        ).astype(BF16)
        for slot in range(group * chunk, (group + 1) * chunk):
            if slot:
                copies.start(
                    final.at[slot], returned.at[seq], home_sems.at[0, slot], ahead(slot), tp
                )

    def mix_b(places):
        span = pl.ds(places[0], len(places))
        which = 0 if places[0] == 0 else 1
        for slot in range(1, n_seq):
            arrived(back_b.at[behind(slot), span], home_sems.at[1 + which, slot])
        for place in places:
            terms = back_b[:, place].reshape(n_seq * 8, width - split)
            mixed_b[:, place] = mixture(place, terms).astype(BF16)

    mix_b((0, 1, 2))
    home(low_order[0])
    home(high_order[0])
    mix_b((3,))
    copies.start(mixed_b.at[1 - core], mixed_pair, attn_sems.at[11], seq, partner)
    for low, high in zip(low_order[1:], high_order[1:]):
        home(low)
        home(high)
    arrived(mixed_pair, attn_sems.at[11])
    for place in (3, 1, 2):
        mixed_sum[place - 1] = (
            mixed_b[core, place].astype(F32) + mixed_pair[place].astype(F32)
        ).astype(BF16)
        copies.start(
            mixed_sum.at[place - 1],
            mixed_in_b.at[place - 1],
            attn_sems.at[11 + place],
            seq,
            peer(place, False),
        )
    returned[seq] = final[0]
    total_b = mixed_b[core, 0].astype(F32) + mixed_pair[0].astype(F32)
    for place in (1, 2, 3):
        arrived(mixed_in_b.at[place - 1], attn_sems.at[11 + place])
        total_b = total_b + mixed_in_b[place - 1].astype(F32)
    residual[:, split:] = residual[:, split:] + total_b
    for slot in range(1, n_seq):
        arrived(returned.at[behind(slot)], home_sems.at[0, slot])
    terms = returned[...].reshape(n_seq * 8, split)
    mixed[...] = mixture(0, terms)
    copies.start(mixed.at[1 - core], mixed_in, attn_sems.at[10], seq, partner)
    out[:, split:] = residual[:, split:].astype(BF16)
    arrived(mixed_in, attn_sems.at[10])
    out[:, :split] = (residual[:, :split] + (mixed[core] + mixed_in[...])).astype(BF16)
    copies.drain()


def local(
    stream_in,
    attn_gain,
    w_qkv,
    key_value_cache,
    w_out,
    mlp_gain,
    expert_index,
    gate_weight,
    w_gateup,
    w_down,
):
    n_seq = lax.axis_size("seq")
    n_tp = lax.axis_size("tp")
    n_x = n_tp // 2
    length, width = stream_in.shape
    count = length // n_tp
    hidden = w_down.shape[1]
    columns = w_qkv.shape[2]
    heads_width = w_out.shape[0]
    vmem, dma = pltpu.VMEM, pltpu.SemaphoreType.DMA
    chunks = n_seq // max(1, n_seq // 4)
    split = width * 5 // 8 // 128 * 128
    rest = width - split
    scratch = [
        vmem((width, length), BF16),
        vmem((width, columns), BF16),
        vmem((width, heads_width), BF16),
        vmem((length, 128), BF16),
        vmem((length, 128), BF16),
        vmem((n_tp, count, width), BF16),
        vmem((n_tp, 2 * TOPK, count), F32),
        vmem((n_x, 2, 2, count // 2, width), BF16),
        vmem((n_x, 2, count // 2, width), BF16),
        vmem((n_x, 2, count // 2, width), BF16),
        vmem((2, count // 2, width), BF16),
        vmem((2, 2, count // 2, width), BF16),
        vmem((count, width), F32),
        vmem((2, count, split), BF16),
        vmem((n_tp, count, rest), BF16),
        vmem((n_x, n_seq * 8, 6 * count), BF16),
        vmem((n_seq, 8, split), BF16),
        vmem((n_seq, n_x, 8, rest), BF16),
        vmem((2, n_x, n_seq, 8, split), BF16),
        vmem((2, n_seq, n_x, 8, rest), BF16),
        vmem((2, 2, hidden, width), BF16),
        vmem((2, hidden, width), BF16),
        vmem((2, 3, 2, n_seq * 8, hidden), F32),
        vmem((2, n_x, n_seq, 8, split), BF16),
        vmem((2, n_seq, n_x, 8, rest), BF16),
        vmem((n_x, n_seq, 8, split), BF16),
        vmem((n_seq, n_x, 8, rest), BF16),
        vmem((n_x, n_seq, 8, split), BF16),
        vmem((n_seq, n_x, 8, rest), BF16),
        vmem((n_seq, 8, split), BF16),
        vmem((2, n_seq, 8, split), BF16),
        vmem((n_seq, 8, split), BF16),
        vmem((n_seq, 8, split), BF16),
        vmem((n_seq, n_x, 8, rest), BF16),
        vmem((2, n_x, count, rest), BF16),
        vmem((n_x, count, rest), BF16),
        vmem((3, count, rest), BF16),
        vmem((3, count, rest), BF16),
        vmem((2, count, split), F32),
        vmem((count, split), F32),
        dma((7,)),
        dma((256,)),
        dma((15,)),
        dma((n_tp,)),
        dma((n_tp,)),
        dma((2, chunks)),
        dma((3, chunks)),
        dma((5, chunks)),
        dma((4, chunks)),
        dma((chunks,)),
        dma((2, chunks)),
        dma((3, n_seq)),
        dma((4,)),
    ]
    in_vmem = pl.BlockSpec(memory_space=pltpu.VMEM)
    return pl.pallas_call(
        functools.partial(layer_kernel, n_seq, n_x),
        out_shape=jax.ShapeDtypeStruct((count, width), BF16),
        in_specs=[in_vmem] * 5 + [pl.BlockSpec(memory_space=pl.ANY)] * 5,
        out_specs=in_vmem,
        scratch_shapes=scratch,
        compiler_params=pltpu.CompilerParams(
            collective_id=0, has_side_effects=True, vmem_limit_bytes=63 * 1024 * 1024
        ),
    )(
        expert_index.T,
        gate_weight.T,
        attn_gain,
        mlp_gain,
        key_value_cache.reshape(length, 128),
        stream_in.T,
        w_qkv.reshape(width, columns),
        w_out.T,
        w_gateup.transpose(0, 2, 3, 1),
        w_down,
    )


def solution(mesh):
    in_specs = (
        P("seq", None),
        P(),
        P(None, "tp", None),
        P(None, "tp", None),
        P("tp", None),
        P(),
        P(("seq", "tp"), None),
        P(("seq", "tp"), None),
        P("seq", None, None, "tp"),
        P("seq", "tp", None),
    )
    out_specs = P(("seq", "tp"), None)
    return jax.shard_map(local, mesh=mesh, in_specs=in_specs, out_specs=out_specs, check_vma=False)
```

```python
import functools

import jax
import jax.numpy as jnp
from jax import lax
from jax.experimental import pallas as pl
from jax.experimental.pallas import tpu as pltpu
from jax.sharding import PartitionSpec as P

HEAD_SIZE = 64
WINDOW_KEYS = 128
TOPK = 4
EPS = 1e-05
MESH = pl.DeviceIdType.MESH
BF16, F32 = jnp.bfloat16, jnp.float32


def rms_scale(values, gain_vec):
    mean_sq = jnp.mean(values * values, axis=-1, keepdims=True)
    return values * lax.rsqrt(mean_sq + EPS) * gain_vec


def contract_last(a, b):
    return lax.dot_general(a, b, (((1,), (1,)), ((), ())), preferred_element_type=F32)


def contract_first(a, b):
    return lax.dot_general(a, b, (((0,), (0,)), ((), ())), preferred_element_type=F32)


class Copies:
    def __init__(self, send_sems):
        self.send_sems = send_sems
        self.started = []

    def start(self, src, dst, recv_sem, seq, tp):
        copy = pltpu.make_async_remote_copy(
            src_ref=src,
            dst_ref=dst,
            send_sem=self.send_sems.at[len(self.started)],
            recv_sem=recv_sem,
            device_id=(seq, tp),
            device_id_type=MESH,
        )
        copy.start()
        self.started.append(copy)

    def drain(self):
        for copy in self.started:
            copy.wait_send()


def arrived(ref, sem):
    pltpu.make_async_copy(ref, ref, sem).wait()


def key_value_sides(keyval):
    keyval = keyval.astype(F32)
    swapped = pltpu.roll(keyval, 64, 1)
    low = lax.broadcasted_iota(jnp.int32, keyval.shape, 1) < HEAD_SIZE
    keys = [jnp.where(low, keyval, 0.0).astype(BF16), jnp.where(low, 0.0, swapped).astype(BF16)]
    values = [jnp.where(low, swapped, 0.0).astype(BF16), jnp.where(low, 0.0, keyval).astype(BF16)]
    return keys, values


def own_scores(projected):
    length = projected.shape[0]
    pairs = projected.shape[1] // 128 - 1
    keys, values = key_value_sides(projected[:, pairs * 128 :])
    queries = jnp.concatenate(
        [projected[:, pair * 128 : (pair + 1) * 128] for pair in range(pairs)], axis=0
    )
    shape = (queries.shape[0], length)
    row = lax.broadcasted_iota(jnp.int32, shape, 0) % length
    later = lax.broadcasted_iota(jnp.int32, shape, 1) > row
    scores = [
        jnp.where(later, -1e30, contract_last(queries, key) * HEAD_SIZE ** (-0.5)) for key in keys
    ]
    return queries, later, scores, values


def window_attention(prepared, earlier):
    queries, later, own, own_values = prepared
    keys, values = key_value_sides(earlier)
    attended = None
    for side in range(2):
        before = contract_last(queries, keys[side]) * HEAD_SIZE ** (-0.5)
        scores = jnp.concatenate([jnp.where(later, before, -1e30), own[side]], axis=1)
        exponent = jnp.exp(scores - jnp.max(scores, axis=-1, keepdims=True))
        weights = (exponent * (1.0 / jnp.sum(exponent, axis=-1, keepdims=True))).astype(BF16)
        both = jnp.concatenate([values[side], own_values[side]], axis=0)
        term = jnp.dot(weights, both, preferred_element_type=F32)
        attended = term if attended is None else attended + term
    attended = attended.astype(BF16)
    length = earlier.shape[0]
    return jnp.concatenate(
        [attended[at : at + length] for at in range(0, attended.shape[0], length)], axis=1
    )


def slot_tables(routes, core, n_seq):
    count = routes[0].shape[1]
    route = jnp.concatenate(routes, axis=1)
    shape = (n_seq * 8, route.shape[1])
    line = lax.broadcasted_iota(jnp.int32, shape, 0)
    token = lax.broadcasted_iota(jnp.int32, shape, 1)
    expert = (line // 8 * 2 + core).astype(F32)
    chosen = jnp.zeros(shape, F32)
    weight = jnp.zeros(shape, F32)
    for k in range(TOPK):
        named = expert == route[k : k + 1, :]
        chosen = chosen + named.astype(F32)
        weight = weight + jnp.where(named, route[TOPK + k : TOPK + k + 1, :], 0.0)
    square = (shape[1], shape[1])
    one = lax.broadcasted_iota(jnp.int32, square, 0)
    two = lax.broadcasted_iota(jnp.int32, square, 1)
    before = (one < two) & (one // count == two // count)
    rank = jnp.dot(
        chosen.astype(BF16), before.astype(F32).astype(BF16), preferred_element_type=F32
    )
    place = (line % 4).astype(F32)
    here = line % 8 // 4 == token // count % 2
    hit = jnp.where(here & (rank == place), chosen, 0.0)
    return hit.astype(BF16), hit * weight


def split3(values):
    high = values.astype(BF16)
    rest = values - high.astype(F32)
    middle = rest.astype(BF16)
    return high, middle, (rest - middle.astype(F32)).astype(BF16)


def layer_kernel(
    n_seq,
    n_x,
    index_own,
    weight_own,
    attn_gain,
    mlp_gain,
    cache,
    stream_hbm,
    w_qkv_hbm,
    w_out_hbm,
    w_gateup_hbm,
    w_down_hbm,
    out,
    stream_t,
    w_qkv,
    w_out,
    tail,
    earlier,
    stream,
    route,
    part,
    attn_pair,
    attn_sum,
    attn_opp,
    attn_in,
    residual,
    hidden_a,
    hidden_b,
    pickers,
    packed_a,
    packed_b,
    rows,
    rows_b,
    w_gateup,
    w_down,
    sums,
    product,
    product_b,
    from_pair,
    from_pair_b,
    chip_sum,
    chip_b,
    ring_opp,
    ring_in,
    final,
    returned,
    back_b,
    mixed_b,
    mixed_pair,
    mixed_sum,
    mixed_in_b,
    mixed,
    mixed_in,
    load_sems,
    send_sems,
    attn_sems,
    route_sems,
    hidden_sems,
    block_sems,
    ring_sems,
    pair_sems,
    back_sems,
    opp_sems,
    in_sems,
    home_sems,
    mix_sems,
):
    seq, tp = lax.axis_index("seq"), lax.axis_index("tp")
    x, core = tp // 2, tp % 2
    nz = 4 if n_seq % 4 == 0 else n_seq
    ny = n_seq // nz
    y, z = seq // nz, seq % nz
    partner = tp + 1 - 2 * core
    right_x, left_x, far_x = (x + 1) % n_x, (x + n_x - 1) % n_x, (x + 2) % n_x
    right, left, far = right_x * 2 + core, left_x * 2 + core, far_x * 2 + core
    chunk = max(1, n_seq // 4)
    chunks = n_seq // chunk
    half = chunks // 2
    y_steps = [0, 2, 1, 3] if ny == 4 else list(range(ny))
    first_order = [0, 2, 3, 1] if chunks == 4 else list(range(chunks))
    low_order = list(range(half))[::-1]
    high_order = list(range(half, chunks))
    width = out.shape[-1]
    split = rows.shape[-1]
    length = stream.shape[0] * stream.shape[1]
    copies = Copies(send_sems)

    def load(src, dst, index):
        copy = pltpu.make_async_copy(src, dst, load_sems.at[index])
        copy.start()
        return copy

    edges = [0, width // 3 // 128 * 128, width * 2 // 3 // 128 * 128, width]
    spans = [pl.ds(a, b - a) for a, b in zip(edges[:-1], edges[1:]) if b > a]
    stream_load = load(stream_hbm, stream_t, 0)
    qkv_loads = [
        load(w_qkv_hbm.at[span], w_qkv.at[span], 1 + i) for i, span in enumerate(spans)
    ]
    out_load = load(w_out_hbm, w_out, 4)

    def behind(slot):
        dy, dz = y_steps[slot // nz], slot % nz
        return ((y + ny - dy) % ny) * nz + (z + nz - dz) % nz

    def ahead(slot):
        dy, dz = y_steps[slot // nz], slot % nz
        return ((y + dy) % ny) * nz + (z + dz) % nz

    order = (x, left_x, right_x, far_x)

    def peer(place, other):
        return order[place] * 2 + (1 - core if other else core)

    peers = [peer(place, other) for place in range(4) for other in (True, False)]
    peers = peers[:1] + peers[2:]

    barrier = pltpu.get_barrier_semaphore()
    after = (seq + 1) % n_seq
    for slot in range(1, n_seq):
        pl.semaphore_signal(barrier, inc=1, device_id=(ahead(slot), tp), device_id_type=MESH)
    for other in peers:
        pl.semaphore_signal(barrier, inc=1, device_id=(seq, other), device_id_type=MESH)
    route[tp, 0:TOPK] = index_own[...].astype(F32)
    route[tp, TOPK:] = weight_own[...]

    square = lax.broadcasted_iota(jnp.int32, (length, length), 0)
    eye = (square == lax.broadcasted_iota(jnp.int32, (length, length), 1)).astype(BF16)
    stream_load.wait()
    tokens = contract_last(eye, stream_t[...])
    stream[...] = tokens.astype(BF16).reshape(stream.shape)
    normed = rms_scale(tokens, attn_gain[...].reshape(1, -1)).astype(BF16)
    projected = None
    for span, (a, b), copy in zip(spans, zip(edges[:-1], edges[1:]), qkv_loads):
        copy.wait()
        term = jnp.dot(normed[:, a:b], w_qkv[span], preferred_element_type=F32)
        projected = term if projected is None else projected + term
    projected = projected.astype(BF16)
    tail[...] = projected[:, projected.shape[1] - 128 :]
    pl.semaphore_wait(barrier, n_seq - 1 + len(peers))
    copies.start(tail, earlier, attn_sems.at[0], after, tp)
    for other in peers:
        copies.start(route.at[tp], route.at[tp], route_sems.at[tp], seq, other)
    prepared = own_scores(projected)
    arrived(earlier, attn_sems.at[0])
    attended = window_attention(prepared, jnp.where(seq == 0, cache[...], earlier[...]))
    out_load.wait()
    weight_loads = [load(w_gateup_hbm, w_gateup, 5), load(w_down_hbm, w_down, 6)]
    part[...] = contract_last(attended, w_out[...]).reshape(part.shape).astype(BF16)

    copies.start(part.at[:, 1 - core], attn_pair, attn_sems.at[2], seq, partner)
    for other in peers:
        arrived(route.at[other], route_sems.at[other])
    placer, weighted = slot_tables(
        [route[order[place] * 2 + c] for place in range(4) for c in range(2)], core, n_seq
    )
    wide = 2 * out.shape[0]
    placers = [placer[:, place * wide : (place + 1) * wide] for place in range(4)]
    pieces = split3(weighted)
    for place in range(4):
        pickers[place] = jnp.concatenate(
            [piece[:, place * wide : (place + 1) * wide] for piece in pieces], axis=1
        )
    arrived(attn_pair, attn_sems.at[2])

    def pair_total(peer_x):
        return part[peer_x, core].astype(F32) + attn_pair[peer_x].astype(F32)

    attn_sum[far_x] = pair_total(far_x).astype(BF16)
    copies.start(attn_sum.at[far_x, 0], attn_opp.at[0], attn_sems.at[3], seq, right)
    copies.start(attn_sum.at[far_x, 1], attn_opp.at[1], attn_sems.at[4], seq, left)
    attn_sum[right_x] = pair_total(right_x).astype(BF16)
    copies.start(attn_sum.at[right_x, 1], attn_in.at[0, 1], attn_sems.at[5], seq, right)
    attn_sum[left_x] = pair_total(left_x).astype(BF16)
    copies.start(attn_sum.at[left_x, 0], attn_in.at[1, 0], attn_sems.at[6], seq, left)
    total = stream[tp].astype(F32).reshape(2, -1, width) + pair_total(x)
    arrived(attn_opp.at[0], attn_sems.at[3])
    attn_sum[right_x, 0] = (
        attn_sum[right_x, 0].astype(F32) + attn_opp[0].astype(F32)
    ).astype(BF16)
    copies.start(attn_sum.at[right_x, 0], attn_in.at[0, 0], attn_sems.at[7], seq, right)
    arrived(attn_opp.at[1], attn_sems.at[4])
    attn_sum[left_x, 1] = (
        attn_sum[left_x, 1].astype(F32) + attn_opp[1].astype(F32)
    ).astype(BF16)
    copies.start(attn_sum.at[left_x, 1], attn_in.at[1, 1], attn_sems.at[8], seq, left)
    for which, part_of, sem in ((0, 1, 5), (1, 0, 6), (0, 0, 7), (1, 1, 8)):
        arrived(attn_in.at[which, part_of], attn_sems.at[sem])
    total = (total + attn_in[0].astype(F32) + attn_in[1].astype(F32)).reshape(-1, width)
    residual[...] = total
    normed = rms_scale(total, mlp_gain[...].reshape(1, -1)).astype(BF16)
    hidden_a[core] = normed[:, :split]
    hidden_b[tp] = normed[:, split:]
    copies.start(hidden_a.at[core], hidden_a.at[core], attn_sems.at[9], seq, partner)
    for other in peers:
        copies.start(hidden_b.at[tp], hidden_b.at[tp], hidden_sems.at[tp], seq, other)
    arrived(hidden_a.at[1 - core], attn_sems.at[9])

    def pack(place, both):
        taken = jnp.dot(
            placers[place], both.reshape(wide, -1), preferred_element_type=F32
        )
        return taken.reshape(n_seq, 8, -1).astype(BF16)

    packed_a[...] = pack(0, hidden_a[...])
    for group in first_order:
        for slot in range(group * chunk, (group + 1) * chunk):
            if slot:
                holder = behind(slot)
                copies.start(
                    packed_a.at[holder], rows.at[core, x, slot], block_sems.at[0, group], holder, tp
                )
    rows[core, x, 0] = packed_a[seq]
    for other in peers:
        arrived(hidden_b.at[other], hidden_sems.at[other])
    for place in range(4):
        packed_b[:, place] = pack(place, hidden_b[pl.ds(order[place] * 2, 2)])
    for group in first_order:
        for slot in range(group * chunk, (group + 1) * chunk):
            if slot:
                holder = behind(slot)
                copies.start(
                    packed_b.at[holder], rows_b.at[core, slot], block_sems.at[1, group], holder, tp
                )
    rows_b[core, 0] = packed_b[seq]

    def slots(group):
        return pl.ds(group * chunk, chunk)

    def spread(group):
        first = 1 if group == 0 else 0
        if chunk > first:
            got = rows.at[core, x, pl.ds(group * chunk + first, chunk - first)]
            arrived(got, block_sems.at[0, group])
        own = rows.at[core, x, slots(group)]
        copies.start(own, own, ring_sems.at[0, group], seq, right)
        copies.start(own, own, ring_sems.at[1, group], seq, left)
        copies.start(own, own, pair_sems.at[0, group], seq, partner)

    done = set()

    def take(from_left, group):
        if (from_left, group) in done:
            return
        done.add((from_left, group))
        got = rows.at[core, left_x if from_left else right_x, slots(group)]
        arrived(got, ring_sems.at[0 if from_left else 1, group])
        if from_left and group < half:
            copies.start(got, got, ring_sems.at[2, group], seq, right)
        if not from_left and group >= half:
            copies.start(got, got, ring_sems.at[2, group], seq, left)
        copies.start(got, got, pair_sems.at[1 if from_left else 2, group], seq, partner)

    def take_b(group):
        first = 1 if group == 0 else 0
        if chunk > first:
            got = rows_b.at[core, pl.ds(group * chunk + first, chunk - first)]
            arrived(got, block_sems.at[1, group])
        own = rows_b.at[core, slots(group)]
        copies.start(own, own, pair_sems.at[4, group], seq, partner)

    def taken_a(expert, places):
        return jnp.concatenate(
            [rows[expert, order[place]].reshape(n_seq * 8, split) for place in places], axis=0
        )

    def taken_b(expert, places):
        return jnp.concatenate(
            [rows_b[expert, :, place].reshape(n_seq * 8, width - split) for place in places], axis=0
        )

    def enter(place):
        for group in range(chunks):
            arrived(rows.at[1 - core, order[place], slots(group)], pair_sems.at[place, group])

    def early(places):
        for place in places:
            enter(place)
        lines = pl.ds(places[0] * n_seq * 8, len(places) * n_seq * 8)

        def one(expert, carry):
            taken = taken_a(expert, places)
            for which in range(2):
                sums[expert, which, lines] = contract_last(
                    taken, w_gateup[expert, which, :, 0:split]
                )
            return carry

        lax.fori_loop(0, 2, one, 0)

    def finish(places, expert, ready):
        taken = taken_b(expert, places)
        gate = contract_last(taken, w_gateup[expert, 0, :, split:])
        up = contract_last(taken, w_gateup[expert, 1, :, split:])
        if ready:
            gate, up = gate + sums[expert, 0], up + sums[expert, 1]
        else:
            taken = taken_a(expert, places)
            gate = gate + contract_last(taken, w_gateup[expert, 0, :, 0:split])
            up = up + contract_last(taken, w_gateup[expert, 1, :, 0:split])
        activated = (gate / (1.0 + jnp.exp(-gate)) * up).astype(BF16)
        for a, b, target in ((0, split, product), (split, width, product_b)):
            result = jnp.dot(activated, w_down[expert, :, a:b], preferred_element_type=F32)
            result = result.reshape(len(places), n_seq, 8, b - a).astype(BF16)
            for at, place in enumerate(places):
                if a == 0:
                    target[expert, order[place]] = result[at]
                else:
                    target[expert, :, place] = result[at]

    def block(places, ready):
        finish(places, 1 - core, ready)
        for place in places:
            block_x = order[place]
            for group in range(chunks):
                copies.start(
                    product.at[1 - core, block_x, slots(group)],
                    from_pair.at[block_x, slots(group)],
                    back_sems.at[place, group],
                    seq,
                    partner,
                )
            copies.start(
                product_b.at[1 - core, :, place],
                from_pair_b.at[:, place],
                mix_sems.at[place],
                seq,
                partner,
            )
        finish(places, core, ready)

    def pair_sum_b(places):
        for place in places:
            arrived(from_pair_b.at[:, place], mix_sems.at[place])
            chip_b[:, place] = (
                product_b[core, :, place].astype(F32) + from_pair_b[:, place].astype(F32)
            ).astype(BF16)
        span = pl.ds(places[0], len(places))
        which = 0 if places[0] == 0 else 1
        for group in first_order:
            for slot in range(group * chunk, (group + 1) * chunk):
                if slot:
                    copies.start(
                        chip_b.at[slot, span],
                        back_b.at[seq, span],
                        home_sems.at[1 + which, slot],
                        ahead(slot),
                        tp,
                    )
        back_b[seq, span] = chip_b[0, span]

    def pair_sum(block_x, which, group):
        at = slots(group)
        arrived(from_pair.at[block_x, at], back_sems.at[which, group])
        chip_sum[block_x, at] = (
            product[core, block_x, at].astype(F32) + from_pair[block_x, at].astype(F32)
        ).astype(BF16)

    for group in first_order:
        spread(group)
    take(True, 0)
    take(False, half)
    take(False, chunks - 1)
    for copy in weight_loads:
        copy.wait()
    early((0,))
    for group in first_order:
        take(True, group)
        take(False, group)
    for group in first_order:
        take_b(group)
    early((1, 2))
    for group in first_order:
        arrived(rows_b.at[1 - core, slots(group)], pair_sems.at[4, group])
    def take_far(group):
        got = rows.at[core, far_x, slots(group)]
        arrived(got, ring_sems.at[2, group])
        copies.start(got, got, pair_sems.at[3, group], seq, partner)

    for group in first_order[:-1]:
        take_far(group)
    block((0, 1, 2), True)
    for group in high_order:
        pair_sum(right_x, 2, group)
        copies.start(
            chip_sum.at[right_x, slots(group)],
            ring_in.at[0, slots(group)],
            in_sems.at[0, group],
            seq,
            right,
        )
    for group in low_order:
        pair_sum(left_x, 1, group)
        copies.start(
            chip_sum.at[left_x, slots(group)],
            ring_in.at[1, slots(group)],
            in_sems.at[1, group],
            seq,
            left,
        )
    take_far(first_order[-1])
    pair_sum_b((0, 1, 2))
    enter(3)
    block((3,), False)
    for low, high in zip(low_order, high_order):
        pair_sum(far_x, 3, low)
        copies.start(
            chip_sum.at[far_x, slots(low)], ring_opp.at[slots(low)], opp_sems.at[low], seq, right
        )
        pair_sum(far_x, 3, high)
        copies.start(
            chip_sum.at[far_x, slots(high)], ring_opp.at[slots(high)], opp_sems.at[high], seq, left
        )
    pair_sum_b((3,))
    for low, high in zip(low_order, high_order):
        pair_sum(right_x, 2, low)
        pair_sum(left_x, 1, high)
        pair_sum(x, 0, low)
        pair_sum(x, 0, high)
    for low, high in zip(low_order, high_order):
        for group, peer_x, target, side in ((low, right_x, right, 0), (high, left_x, left, 1)):
            at = slots(group)
            arrived(ring_opp.at[at], opp_sems.at[group])
            chip_sum[peer_x, at] = (
                chip_sum[peer_x, at].astype(F32) + ring_opp[at].astype(F32)
            ).astype(BF16)
            copies.start(
                chip_sum.at[peer_x, at], ring_in.at[side, at], in_sems.at[side, group], seq, target
            )

    def mixture(place, terms):
        parts = contract_first(pickers[place], terms)
        whole = parts[:wide] + parts[wide : 2 * wide] + parts[2 * wide :]
        return whole.reshape(2, wide // 2, -1)

    def home(group):
        at = slots(group)
        arrived(ring_in.at[0, at], in_sems.at[0, group])
        arrived(ring_in.at[1, at], in_sems.at[1, group])
        final[at] = (
            chip_sum[x, at].astype(F32) + ring_in[0, at].astype(F32) + ring_in[1, at].astype(F32)
        ).astype(BF16)
        for slot in range(group * chunk, (group + 1) * chunk):
            if slot:
                copies.start(
                    final.at[slot], returned.at[seq], home_sems.at[0, slot], ahead(slot), tp
                )

    def mix_b(places):
        span = pl.ds(places[0], len(places))
        which = 0 if places[0] == 0 else 1
        for slot in range(1, n_seq):
            arrived(back_b.at[behind(slot), span], home_sems.at[1 + which, slot])
        for place in places:
            terms = back_b[:, place].reshape(n_seq * 8, width - split)
            mixed_b[:, place] = mixture(place, terms).astype(BF16)

    mix_b((0, 1, 2))
    home(low_order[0])
    home(high_order[0])
    mix_b((3,))
    copies.start(mixed_b.at[1 - core], mixed_pair, attn_sems.at[11], seq, partner)
    for low, high in zip(low_order[1:], high_order[1:]):
        home(low)
        home(high)
    arrived(mixed_pair, attn_sems.at[11])
    for place in (3, 1, 2):
        mixed_sum[place - 1] = (
            mixed_b[core, place].astype(F32) + mixed_pair[place].astype(F32)
        ).astype(BF16)
        copies.start(
            mixed_sum.at[place - 1],
            mixed_in_b.at[place - 1],
            attn_sems.at[11 + place],
            seq,
            peer(place, False),
        )
    returned[seq] = final[0]
    total_b = mixed_b[core, 0].astype(F32) + mixed_pair[0].astype(F32)
    for place in (1, 2, 3):
        arrived(mixed_in_b.at[place - 1], attn_sems.at[11 + place])
        total_b = total_b + mixed_in_b[place - 1].astype(F32)
    residual[:, split:] = residual[:, split:] + total_b
    for slot in range(1, n_seq):
        arrived(returned.at[behind(slot)], home_sems.at[0, slot])
    terms = returned[...].reshape(n_seq * 8, split)
    mixed[...] = mixture(0, terms)
    copies.start(mixed.at[1 - core], mixed_in, attn_sems.at[10], seq, partner)
    out[:, split:] = residual[:, split:].astype(BF16)
    arrived(mixed_in, attn_sems.at[10])
    out[:, :split] = (residual[:, :split] + (mixed[core] + mixed_in[...])).astype(BF16)
    copies.drain()


def local(
    stream_in,
    attn_gain,
    w_qkv,
    key_value_cache,
    w_out,
    mlp_gain,
    expert_index,
    gate_weight,
    w_gateup,
    w_down,
):
    n_seq = lax.axis_size("seq")
    n_tp = lax.axis_size("tp")
    n_x = n_tp // 2
    length, width = stream_in.shape
    count = length // n_tp
    hidden = w_down.shape[1]
    columns = w_qkv.shape[2]
    heads_width = w_out.shape[0]
    vmem, dma = pltpu.VMEM, pltpu.SemaphoreType.DMA
    chunks = n_seq // max(1, n_seq // 4)
    split = width * 5 // 8 // 128 * 128
    rest = width - split
    scratch = [
        vmem((width, length), BF16),
        vmem((width, columns), BF16),
        vmem((width, heads_width), BF16),
        vmem((length, 128), BF16),
        vmem((length, 128), BF16),
        vmem((n_tp, count, width), BF16),
        vmem((n_tp, 2 * TOPK, count), F32),
        vmem((n_x, 2, 2, count // 2, width), BF16),
        vmem((n_x, 2, count // 2, width), BF16),
        vmem((n_x, 2, count // 2, width), BF16),
        vmem((2, count // 2, width), BF16),
        vmem((2, 2, count // 2, width), BF16),
        vmem((count, width), F32),
        vmem((2, count, split), BF16),
        vmem((n_tp, count, rest), BF16),
        vmem((n_x, n_seq * 8, 6 * count), BF16),
        vmem((n_seq, 8, split), BF16),
        vmem((n_seq, n_x, 8, rest), BF16),
        vmem((2, n_x, n_seq, 8, split), BF16),
        vmem((2, n_seq, n_x, 8, rest), BF16),
        vmem((2, 2, hidden, width), BF16),
        vmem((2, hidden, width), BF16),
        vmem((2, 2, 3 * n_seq * 8, hidden), F32),
        vmem((2, n_x, n_seq, 8, split), BF16),
        vmem((2, n_seq, n_x, 8, rest), BF16),
        vmem((n_x, n_seq, 8, split), BF16),
        vmem((n_seq, n_x, 8, rest), BF16),
        vmem((n_x, n_seq, 8, split), BF16),
        vmem((n_seq, n_x, 8, rest), BF16),
        vmem((n_seq, 8, split), BF16),
        vmem((2, n_seq, 8, split), BF16),
        vmem((n_seq, 8, split), BF16),
        vmem((n_seq, 8, split), BF16),
        vmem((n_seq, n_x, 8, rest), BF16),
        vmem((2, n_x, count, rest), BF16),
        vmem((n_x, count, rest), BF16),
        vmem((3, count, rest), BF16),
        vmem((3, count, rest), BF16),
        vmem((2, count, split), F32),
        vmem((count, split), F32),
        dma((7,)),
        dma((256,)),
        dma((15,)),
        dma((n_tp,)),
        dma((n_tp,)),
        dma((2, chunks)),
        dma((3, chunks)),
        dma((5, chunks)),
        dma((4, chunks)),
        dma((chunks,)),
        dma((2, chunks)),
        dma((3, n_seq)),
        dma((4,)),
    ]
    in_vmem = pl.BlockSpec(memory_space=pltpu.VMEM)
    return pl.pallas_call(
        functools.partial(layer_kernel, n_seq, n_x),
        out_shape=jax.ShapeDtypeStruct((count, width), BF16),
        in_specs=[in_vmem] * 5 + [pl.BlockSpec(memory_space=pl.ANY)] * 5,
        out_specs=in_vmem,
        scratch_shapes=scratch,
        compiler_params=pltpu.CompilerParams(
            collective_id=0, has_side_effects=True, vmem_limit_bytes=63 * 1024 * 1024
        ),
    )(
        expert_index.T,
        gate_weight.T,
        attn_gain,
        mlp_gain,
        key_value_cache.reshape(length, 128),
        stream_in.T,
        w_qkv.reshape(width, columns),
        w_out.T,
        w_gateup.transpose(0, 2, 3, 1),
        w_down,
    )


def solution(mesh):
    in_specs = (
        P("seq", None),
        P(),
        P(None, "tp", None),
        P(None, "tp", None),
        P("tp", None),
        P(),
        P(("seq", "tp"), None),
        P(("seq", "tp"), None),
        P("seq", None, None, "tp"),
        P("seq", "tp", None),
    )
    out_specs = P(("seq", "tp"), None)
    return jax.shard_map(local, mesh=mesh, in_specs=in_specs, out_specs=out_specs, check_vma=False)
```
